256 devices in a mesh: tok: 128 (over x, y, z_lo, core), mem: 2 (over z_hi).
Axes of the slice: x: 4, y: 4, z: 8 (z_hi: 2, z_lo: 4; z = z_hi * 4 + z_lo), core: 2. Of those that a mesh axis runs over, the one named last changes fastest.
Arguments:
- queries: bfloat16 [65536, 1024], P('tok', 'mem'), may hold values from -6 to 6
- keys: bfloat16 [65536, 1024], P('tok', 'mem'), may hold values from -6 to 6
- values: bfloat16 [65536, 1024], P('tok', 'mem'), may hold values from -6 to 6
- step_sizes: float32 [4, 65536], P(None, 'tok'), may hold values from 0.05 to 0.5
- fast_weights: float32 [4, 256, 768], P(None, 'mem'), may hold values from -0.375 to 0.375
- view_lengths: int32 [256], replicated, may hold values from 1 to 512, 65536 in all
Outputs:
- layer_out: bfloat16 [65536, 1024], P('tok', 'mem')
The draws below stay inside these ranges and needn't reach their ends.
Inputs may be any that keep to these rules, and one draw needn't show every extreme that they name: `view_lengths`: the lengths sum to 65536 and the longest view has exactly 512 tokens.
All inputs are finite; a program needn't handle non-finite values.
Results may differ from the reference program's by a relative error of at most 0.011.
Values may be sent and summed in bfloat16 or wider, within the bound.
A program may use at most 64 MiB of HBM per device.

```python
import math
import jax
import jax.numpy as jnp
import numpy as np
from jax import lax

NM = 4
DM = 256
FH = 256
HD = 128
TOK_DEV = 512
D = 1024
HEADS = 8
TOKENS = 65536
VIEWS = 256
N_TOK = 128


def plant_pair(base_key):
    mixed_key = jax.random.fold_in(base_key, 91)
    key_q, key_k = jax.random.split(mixed_key, 2)
    query_draw = jnp.clip(jax.random.normal(key_q, (TOKENS, D), jnp.float32), -6.0, 6.0)
    key_draw = jnp.clip(jax.random.normal(key_k, (TOKENS, D), jnp.float32), -6.0, 6.0)
    return (query_draw, key_draw)


def draw_queries(key, part):
    return plant_pair(key)[0].astype(jnp.bfloat16)


def draw_keys(key, part):
    return plant_pair(key)[1].astype(jnp.bfloat16)


def levels(stream_key, shape, cuts, low, high):
    def one(position, shards_of):
        steps = jax.random.uniform(jax.random.fold_in(jax.random.fold_in(stream_key, 6), position), (shards_of,), jnp.float32, low / len(cuts), high / len(cuts))
        return jnp.repeat(jnp.exp(steps), shape[position] // shards_of).reshape((-1,) + (1,) * (len(shape) - position - 1))

    level = one(*cuts[0])
    for cut in cuts[1:]:
        level = level * one(*cut)
    return level


def profile(number_of, total, reach, lean):
    weights = [(1 << 20) // math.isqrt(grade ** lean) + 1 for grade in range(2, number_of + 1)]
    spare, given = total - reach - (number_of - 1), [1] * (number_of - 1)
    while spare > 0:
        candidates = [i for i in range(number_of - 1) if given[i] < reach]
        pool, remaining = sum([weights[i] for i in candidates]), spare
        for i in candidates:
            extra = min(reach - given[i], max(1, remaining * weights[i] // pool), spare)
            given[i] = given[i] + extra
            spare = spare - extra
    return np.array([reach] + given)


def ragged(rng, number_of, total, limit, lean):
    if number_of == 2:
        one = jax.random.randint(rng, (), max(1, total - limit), min(limit, total - 1) + 1)
        return jnp.stack([one, total - one])
    lengths = jnp.asarray(profile(number_of, total, limit, lean), jnp.int32)
    twos = (number_of - 1) // 2
    source_of, receiver = lengths[1:1 + 2 * twos:2], lengths[2:2 + 2 * twos:2]
    room = jnp.minimum(source_of - 1, limit - receiver)
    passed = jax.random.randint(jax.random.fold_in(rng, 1), (twos,), 0, 1 << 20) % (room + 1)
    lengths = lengths.at[1:1 + 2 * twos:2].set(source_of - passed).at[2:2 + 2 * twos:2].set(receiver + passed)
    return lengths[jax.random.permutation(jax.random.fold_in(rng, 2), number_of)]


def centred(stream_key, dims, deviation, bound, cuts=(), kind=jnp.bfloat16):
    array = jax.random.normal(stream_key, dims, jnp.float32) * deviation
    if len(cuts) > 0:
        array = levels(stream_key, dims, cuts, -0.22, 0.18) * array
    return jnp.clip(array, min=-bound, max=bound).astype(kind)


def setup_inputs(seed: int = 0) -> dict:
    seeds = jax.random.split(jax.random.key(seed), 7)
    queries = draw_queries(jax.random.fold_in(seeds[6], 71), 0)
    keys = draw_keys(jax.random.fold_in(seeds[6], 71), 0)
    values = centred(seeds[2], (TOKENS, D), 1.0, 6.0, ((0, 128), (1, 2)))
    step_sizes = jnp.clip(jnp.exp(math.log(0.5) - 2.3025851 * jax.random.uniform(seeds[3], (NM, TOKENS), jnp.float32) ** levels(seeds[3], (NM, TOKENS), ((1, 128),), -0.2, 0.2)), 0.05, 0.5)
    fast_weights = centred(seeds[4], (NM, FH, 3 * DM), DM ** -0.5, 0.375, ((1, 2),), jnp.float32)
    view_lengths = ragged(seeds[5], VIEWS, TOKENS, TOK_DEV, 2).astype(jnp.int32)
    return {"queries": queries, "keys": keys, "values": values, "step_sizes": step_sizes, "fast_weights": fast_weights, "view_lengths": view_lengths}


norm_epsilon = 1e-06

def silu_pair(pre_act):
    sigmoid_val = jax.nn.sigmoid(pre_act)
    return (pre_act * sigmoid_val, sigmoid_val * (1.0 + pre_act * (1.0 - sigmoid_val)))

def renormed(weights, gradient, step_rate):
    stepped = weights - gradient * step_rate
    shaped = stepped.reshape(stepped.shape[0], 3, DM)
    before = weights.reshape(weights.shape[0], 3, DM)
    old_norm = jnp.sqrt(lax.optimization_barrier(jnp.sum(before * before, axis=2)))
    new_norm = jnp.sqrt(lax.optimization_barrier(jnp.sum(shaped * shaped, axis=2)) + norm_epsilon)
    return (shaped * (old_norm / new_norm)[:, :, None]).reshape(stepped.shape)

def memory_grads(key_part, value_part, token_rates, weights):
    rounded = weights.astype(jnp.bfloat16).astype(jnp.float32)
    weight_in = rounded[:, :DM]
    weight_up = rounded[:, DM:2 * DM]
    weight_out = rounded[:, 2 * DM:]
    key_float = key_part.astype(jnp.float32)
    gate_pre = jnp.einsum('td,fd->tf', key_float, weight_in)
    up_pre = jnp.einsum('td,fd->tf', key_float, weight_up)
    swish_val, slope_val = silu_pair(gate_pre)
    hidden = (swish_val * up_pre).astype(jnp.bfloat16).astype(jnp.float32)
    scaled = (token_rates[:, None] * value_part.astype(jnp.float32)).astype(jnp.bfloat16).astype(jnp.float32)
    grad_out = -jnp.einsum('tf,td->fd', hidden, scaled)
    back_flow = -jnp.einsum('td,fd->tf', scaled, weight_out)
    gate_back = (back_flow * up_pre * slope_val).astype(jnp.bfloat16).astype(jnp.float32)
    up_back = (back_flow * swish_val).astype(jnp.bfloat16).astype(jnp.float32)
    grad_in = jnp.einsum('tf,td->fd', gate_back, key_float)
    grad_up = jnp.einsum('tf,td->fd', up_back, key_float)
    return jnp.concatenate([grad_in, grad_up, grad_out], axis=1)

def memory_read(query_part, weights):
    rounded = weights.astype(jnp.bfloat16).astype(jnp.float32)
    query_float = query_part.astype(jnp.float32)
    gate_pre = jnp.einsum('td,fd->tf', query_float, rounded[:, :DM])
    up_pre = jnp.einsum('td,fd->tf', query_float, rounded[:, DM:2 * DM])
    swish_val, slope_val = silu_pair(gate_pre)
    read_hidden = (swish_val * up_pre).astype(jnp.bfloat16).astype(jnp.float32)
    return jnp.einsum('tf,fd->td', read_hidden, rounded[:, 2 * DM:])

def reference(queries, keys, values, step_sizes, fast_weights, view_lengths):
    view_ids = jnp.repeat(jnp.arange(VIEWS, dtype=jnp.int32), view_lengths, total_repeat_length=TOKENS).astype(jnp.int32)
    edge_fill = jnp.full((TOK_DEV,), -1, jnp.int32)
    padded_views = jnp.concatenate([edge_fill, view_ids, edge_fill])
    zero_rows = jnp.zeros((TOK_DEV, D), keys.dtype)
    padded_keys = jnp.concatenate([zero_rows, keys, zero_rows], axis=0)
    padded_values = jnp.concatenate([zero_rows, values, zero_rows], axis=0)
    score_scale = 1.0 / math.sqrt(HD)

    def one_block(block_index):
        row_start = (block_index * TOK_DEV).astype(jnp.int32)
        query_block = lax.dynamic_slice_in_dim(queries, row_start, TOK_DEV, 0).astype(jnp.float32).reshape(TOK_DEV, HEADS, HD)
        key_block = lax.dynamic_slice_in_dim(padded_keys, row_start, 3 * TOK_DEV, 0).astype(jnp.float32).reshape(3 * TOK_DEV, HEADS, HD)
        value_block = lax.dynamic_slice_in_dim(padded_values, row_start, 3 * TOK_DEV, 0).astype(jnp.float32).reshape(3 * TOK_DEV, HEADS, HD)
        query_views = lax.dynamic_slice_in_dim(view_ids, row_start, TOK_DEV, 0)
        key_views = lax.dynamic_slice_in_dim(padded_views, row_start, 3 * TOK_DEV, 0)
        scores = jnp.einsum('qhd,khd->hqk', query_block, key_block) * score_scale
        same_view = query_views[:, None] == key_views[None, :]
        scores = jnp.where(same_view[None], scores, -1e+30)
        row_peak = lax.optimization_barrier(jnp.max(scores, axis=2, keepdims=True))
        exponent = jnp.exp(scores - row_peak)
        probs = (exponent / lax.optimization_barrier(jnp.sum(exponent, axis=2, keepdims=True))).astype(jnp.bfloat16).astype(jnp.float32)
        output = jnp.einsum('hqk,khd->qhd', probs, value_block)
        return output.reshape(TOK_DEV, D)
    attended = lax.map(one_block, jnp.arange(N_TOK, dtype=jnp.int32)).reshape(TOKENS, D)
    step_rate = 1.0 / math.sqrt(TOKENS)
    pieces = []
    for memory in range(NM):
        first = memory * DM
        gradient = memory_grads(keys[:, first:first + DM], values[:, first:first + DM], step_sizes[memory], fast_weights[memory])
        updated = renormed(fast_weights[memory], gradient, step_rate)
        pieces.append(memory_read(queries[:, first:first + DM], updated))
    return (attended + jnp.concatenate(pieces, axis=1)).astype(jnp.bfloat16)
```

```python
import math

import jax
import jax.numpy as jnp
from jax import lax
from jax.experimental import pallas as pl
from jax.experimental.pallas import tpu as pltpu
from jax.sharding import PartitionSpec as P

DM = 256
HD = 128
PLANE = 16
COLUMN = 4
UNITS = 128
PIECE = UNITS // PLANE
WIDE = 3 * DM
MESH = pl.DeviceIdType.MESH
NT = (((1,), (1,)), ((), ()))
NN = (((1,), (0,)), ((), ()))

norm_epsilon = 1e-06


def dot(a, b, dims):
    return lax.dot_general(a, b, dims, preferred_element_type=jnp.float32)


def flat(pieces):
    return pieces.astype(jnp.float32).reshape(UNITS, WIDE)


def body(
    q_ref, k_ref, v_ref, step_ref, fw_ref, len_ref, out_ref,
    kx, vx, acc, kid, qid,
    cross, wo, part, inbox, piece_out, piece_in, col_out, col_in, nw,
    sems, half_sems, halo_sems,
):
    tok = lax.axis_index("tok")
    mem = lax.axis_index("mem")
    n_tok = lax.axis_size("tok")
    rows = q_ref.shape[0]
    core = lax.rem(tok, 2)
    other = 1 - core
    plane = tok // 8
    spot = lax.rem(tok, 8)
    level = spot // 2
    partner = tok + 1 - 2 * core
    right = lax.rem(tok + 1, n_tok)
    left = lax.rem(tok + n_tok - 1, n_tok)
    total_rows = n_tok * rows
    rate = 1.0 / math.sqrt(total_rows)

    def plane_peer(d):
        return lax.rem(plane + d, PLANE) * 8 + spot

    def column_peer(d):
        return plane * 8 + lax.rem(level + d, COLUMN) * 2 + core

    def send(src, dst, s_sem, r_sem, tok_id, mem_id=None):
        return pltpu.make_async_remote_copy(
            src_ref=src, dst_ref=dst, send_sem=s_sem, recv_sem=r_sem,
            device_id={"tok": tok_id, "mem": mem if mem_id is None else mem_id},
            device_id_type=MESH,
        )

    own_k = pltpu.make_async_copy(k_ref, kx.at[pl.ds(rows, rows)], sems.at[0])
    own_v = pltpu.make_async_copy(v_ref, vx.at[pl.ds(rows, rows)], sems.at[1])
    own_k.start()
    own_v.start()

    barrier = pltpu.get_barrier_semaphore()

    def greet(tok_id, mem_id):
        pl.semaphore_signal(
            barrier, inc=1, device_id={"tok": tok_id, "mem": mem_id}, device_id_type=MESH
        )

    greet(partner, mem)
    greet(tok, 1 - mem)
    greet(left, mem)
    greet(right, mem)

    @pl.loop(1, PLANE)
    def _(d):
        greet(plane_peer(d), mem)

    @pl.loop(1, COLUMN)
    def _(d):
        greet(column_peer(d), mem)

    own_k.wait()
    own_v.wait()

    def grads(j, wb):
        lanes = pl.ds(pl.multiple_of(j * DM, DM), DM)
        kj = kx[pl.ds(rows, rows), lanes]
        vj = vx[pl.ds(rows, rows), lanes]
        step = step_ref[pl.ds(2 * mem + j, 1), :]
        pre = dot(jnp.concatenate([wb[:, :DM], wb[:, DM : 2 * DM]], axis=0), kj, NT)
        gate, up = pre[:UNITS], pre[UNITS:]
        back = -dot(wb[:, 2 * DM :], vj, NT) * step
        sig = jax.nn.sigmoid(gate)
        swish = gate * sig
        slope = sig * (1.0 + gate * (1.0 - sig))
        hidden = (swish * up * step).astype(jnp.bfloat16)
        gate_back = (back * up * slope).astype(jnp.bfloat16)
        up_back = (back * swish).astype(jnp.bfloat16)
        both = dot(jnp.concatenate([gate_back, up_back], axis=0), kj, NN)
        out = -dot(hidden, vj, NN)
        return jnp.concatenate([both[:UNITS], both[UNITS:], out], axis=1).reshape(
            PLANE, PIECE, WIDE
        )

    def core_start(half, value):
        part[half, 0] = value.astype(jnp.bfloat16)
        copy = send(part.at[half, 0], inbox.at[half], half_sems.at[half, 0], half_sems.at[half, 1], partner)
        copy.start()
        return copy

    def scatter_start(half, copy, own):
        copy.wait_recv()
        total = own[...] + inbox[half].astype(jnp.float32)
        own[...] = total
        part[half, 1] = total.astype(jnp.bfloat16)

        @pl.loop(1, PLANE)
        def _(d):
            to = lax.rem(plane + d, PLANE)
            send(
                part.at[half, 1, to], piece_in.at[half, d - 1],
                half_sems.at[half, 2], half_sems.at[half, 3], to * 8 + spot,
            ).start()

    def whole(half):
        return send(
            part.at[half, 1, pl.ds(0, PLANE - 1)], piece_in.at[half],
            half_sems.at[half, 2], half_sems.at[half, 3], plane_peer(1),
        )

    def column_start(half, own):
        whole(half).wait_recv()
        total = own[plane]
        for d in range(PLANE - 1):
            total = total + piece_in[half, d].astype(jnp.float32)
        col_out[half] = total

        @pl.loop(1, COLUMN)
        def _(d):
            send(
                col_out.at[half], col_in.at[half, d - 1],
                half_sems.at[half, 4], half_sems.at[half, 5], column_peer(d),
            ).start()

    def column_whole(half):
        return send(
            col_in.at[half], col_in.at[half],
            half_sems.at[half, 4], half_sems.at[half, 5], column_peer(1),
        )

    def update(half, before):
        column_whole(half).wait_recv()
        total = col_out[half]
        for d in range(COLUMN - 1):
            total = total + col_in[half, d]
        stepped = before - total * rate
        blocks = []
        for b in range(3):
            old = before[:, b * DM : (b + 1) * DM]
            new = stepped[:, b * DM : (b + 1) * DM]
            old_norm = jnp.sqrt(jnp.sum(old * old, axis=1, keepdims=True))
            new_norm = jnp.sqrt(jnp.sum(new * new, axis=1, keepdims=True) + norm_epsilon)
            blocks.append(new * (old_norm / new_norm))
        nw[half, core, plane] = jnp.concatenate(blocks, axis=1).astype(jnp.bfloat16)

        @pl.loop(1, PLANE)
        def _(d):
            send(
                nw.at[half, core, plane], nw.at[half, core, plane],
                half_sems.at[half, 6], half_sems.at[half, 7], plane_peer(d),
            ).start()

    def gather_whole(half):
        return send(
            nw.at[half, core, pl.ds(0, PLANE - 1)], nw.at[half, core, pl.ds(0, PLANE - 1)],
            half_sems.at[half, 6], half_sems.at[half, 7], plane_peer(1),
        )

    def swap_start(half):
        gather_whole(half).wait_recv()
        copy = send(
            nw.at[half, core], nw.at[half, core],
            half_sems.at[half, 8], half_sems.at[half, 9], partner,
        )
        copy.start()
        return copy

    own_l, own_o = piece_out.at[0], piece_out.at[1]

    away = grads(other, fw_ref[2 * mem + other].astype(jnp.bfloat16))
    own_l[...] = grads(core, fw_ref[2 * mem + core].astype(jnp.bfloat16))

    pl.semaphore_wait(barrier, PLANE - 1 + COLUMN - 1 + 4)

    first = pl.ds(pl.multiple_of(plane * PIECE, PIECE), PIECE)
    crossing = send(
        fw_ref.at[2 * (1 - mem) + core, first], cross,
        sems.at[2], sems.at[3], tok, 1 - mem,
    )
    crossing.start()
    core_l = core_start(0, away)

    halos = []
    middle = pl.ds(rows, rows)
    for n, buf in enumerate((kx, vx)):
        halos.append(send(buf.at[middle], buf.at[pl.ds(0, rows)], halo_sems.at[n, 0], halo_sems.at[n, 1], right))
        halos.append(send(buf.at[middle], buf.at[pl.ds(2 * rows, rows)], halo_sems.at[n, 2], halo_sems.at[n, 3], left))
    for copy in halos:
        copy.start()

    scatter_start(0, core_l, own_l)

    crossing.wait_recv()
    wo[core, plane] = cross[...].astype(jnp.bfloat16)

    @pl.loop(1, PLANE)
    def _(d):
        send(
            wo.at[core, plane], wo.at[core, plane], sems.at[4], sems.at[5], plane_peer(d)
        ).start()

    count = len_ref.shape[1]
    lengths = len_ref[...].astype(jnp.float32)
    square = (count, count)
    down = lax.broadcasted_iota(jnp.int32, square, 0)
    along = lax.broadcasted_iota(jnp.int32, square, 1)
    spread = jnp.broadcast_to(lengths, square)
    ends_col = jnp.sum(jnp.where(along <= down, spread, 0.0), axis=1, keepdims=True)
    len_col = jnp.sum(jnp.where(along == down, spread, 0.0), axis=1, keepdims=True)
    ends_row = jnp.sum(jnp.where(down <= along, len_col, 0.0), axis=0, keepdims=True)
    base = tok * rows
    spots = base - rows + lax.broadcasted_iota(jnp.int32, (1, 3 * rows), 1)
    spots_f = spots.astype(jnp.float32)
    key_views = jnp.sum(jnp.where(ends_col <= spots_f, 1.0, 0.0), axis=0, keepdims=True)
    kid[...] = jnp.where((spots >= 0) & (spots < total_rows), key_views, -1.0)
    rows_f = (base + lax.broadcasted_iota(jnp.int32, (rows, 1), 0)).astype(jnp.float32)
    query_views = jnp.sum(jnp.where(ends_row <= rows_f, 1.0, 0.0), axis=1, keepdims=True)
    qid[...] = jnp.broadcast_to(query_views, (rows, HD))

    gathered = send(
        wo.at[core, pl.ds(0, PLANE - 1)], wo.at[core, pl.ds(0, PLANE - 1)],
        sems.at[4], sems.at[5], plane_peer(1),
    )
    gathered.wait_recv()
    swapped = send(wo.at[core], wo.at[core], sems.at[6], sems.at[7], partner)
    swapped.start()

    own_o[...] = grads(core, flat(wo[core]).astype(jnp.bfloat16))
    swapped.wait_recv()
    core_o = core_start(1, grads(other, flat(wo[other]).astype(jnp.bfloat16)))

    column_start(0, own_l)
    scatter_start(1, core_o, own_o)
    update(0, fw_ref[2 * mem + core, first])
    column_start(1, own_o)
    swap_l = swap_start(0)
    update(1, cross[...])

    for copy in halos:
        copy.wait_recv()

    factor = 1.0 / math.sqrt(HD) * math.log2(math.e)
    heads = q_ref.shape[1] // HD
    reach = rows + rows + HD

    @pl.loop(0, rows // HD)
    def _(i):
        here = pl.ds(pl.multiple_of(i * HD, HD), HD)
        keys = pl.ds(pl.multiple_of(i * HD, HD), reach)
        same = qid[here, :1] == kid[:, keys]
        for h in range(heads):
            lanes = slice(h * HD, (h + 1) * HD)
            scores = dot(q_ref[here, lanes], kx[keys, lanes], NT)
            scores = jnp.where(same, scores * factor, -1e30)
            peak = jnp.max(scores, axis=1, keepdims=True)
            weight = jnp.exp2(scores - peak)
            mass = jnp.sum(weight, axis=1, keepdims=True)
            acc[here, lanes] = dot(weight.astype(jnp.bfloat16), vx[keys, lanes], NN) / mass

    swap_l.wait_recv()
    swap_o = swap_start(1)

    def read(half, j):
        w = flat(nw[half, j]).astype(jnp.bfloat16)
        qj = q_ref[:, j * DM : (j + 1) * DM]
        pre = dot(qj, jnp.concatenate([w[:, :DM], w[:, DM : 2 * DM]], axis=0), NT)
        gate, up = pre[:, :UNITS], pre[:, UNITS:]
        hidden = (gate * jax.nn.sigmoid(gate) * up).astype(jnp.bfloat16)
        return dot(hidden, w[:, 2 * DM :], NN)

    for j in range(2):
        lanes = slice(j * DM, (j + 1) * DM)
        acc[:, lanes] = acc[:, lanes] + read(0, j)
    swap_o.wait_recv()
    for j in range(2):
        lanes = slice(j * DM, (j + 1) * DM)
        out_ref[:, lanes] = (acc[:, lanes] + read(1, j)).astype(jnp.bfloat16)

    crossing.wait_send()
    gathered.wait_send()
    swapped.wait_send()
    for copy in halos:
        copy.wait_send()
    for half, (first_copy, last_copy) in enumerate(((core_l, swap_l), (core_o, swap_o))):
        first_copy.wait_send()
        whole(half).wait_send()
        column_whole(half).wait_send()
        gather_whole(half).wait_send()
        last_copy.wait_send()


def on_device(queries, keys, values, step_sizes, fast_weights, view_lengths):
    rows, feats = queries.shape
    vmem = pl.BlockSpec(memory_space=pltpu.VMEM)
    hbm = pl.BlockSpec(memory_space=pl.ANY)
    bf, f32 = jnp.bfloat16, jnp.float32
    pieces = (PLANE, PIECE, WIDE)
    return pl.pallas_call(
        body,
        out_shape=jax.ShapeDtypeStruct((rows, feats), bf),
        in_specs=[vmem, hbm, hbm, vmem, vmem, vmem],
        out_specs=vmem,
        scratch_shapes=[
            pltpu.VMEM((3 * rows, feats), bf),
            pltpu.VMEM((3 * rows, feats), bf),
            pltpu.VMEM((rows, feats), f32),
            pltpu.VMEM((1, 3 * rows), f32),
            pltpu.VMEM((rows, HD), f32),
            pltpu.VMEM((PIECE, WIDE), f32),
            pltpu.VMEM((2,) + pieces, bf),
            pltpu.VMEM((2, 2) + pieces, bf),
            pltpu.VMEM((2,) + pieces, bf),
            pltpu.VMEM((2,) + pieces, f32),
            pltpu.VMEM((2, PLANE - 1, PIECE, WIDE), bf),
            pltpu.VMEM((2, PIECE, WIDE), f32),
            pltpu.VMEM((2, COLUMN - 1, PIECE, WIDE), f32),
            pltpu.VMEM((2, 2) + pieces, bf),
            pltpu.SemaphoreType.DMA((8,)),
            pltpu.SemaphoreType.DMA((2, 10)),
            pltpu.SemaphoreType.DMA((2, 4)),
        ],
        compiler_params=pltpu.CompilerParams(
            collective_id=0, has_side_effects=True, vmem_limit_bytes=48 * 1024 * 1024
        ),
    )(queries, keys, values, step_sizes, fast_weights, view_lengths.reshape(1, -1))


def solution(mesh):
    placed = (
        P("tok", "mem"),
        P("tok", "mem"),
        P("tok", "mem"),
        P(None, "tok"),
        P(None, "mem", None),
        P(),
    )
    return jax.shard_map(
        on_device, mesh=mesh, in_specs=placed, out_specs=P("tok", "mem"), check_vma=False
    )
```

```python
import math

import jax
import jax.numpy as jnp
from jax import lax
from jax.experimental import pallas as pl
from jax.experimental.pallas import tpu as pltpu
from jax.sharding import PartitionSpec as P

DM = 256
HD = 128
PLANE = 16
COLUMN = 4
UNITS = 128
PIECE = UNITS // PLANE
WIDE = 3 * DM
VMEM_BYTES = 66_000_000
MESH = pl.DeviceIdType.MESH
SIDE = 4
FAR_FIRST = sorted(
    (d for d in range(1, PLANE)),
    key=lambda d: -(min(d // SIDE, SIDE - d // SIDE) + min(d % SIDE, SIDE - d % SIDE)),
)
NT = (((1,), (1,)), ((), ()))
NN = (((1,), (0,)), ((), ()))

norm_epsilon = 1e-06


def dot(a, b, dims):
    return lax.dot_general(a, b, dims, preferred_element_type=jnp.float32)


def flat(pieces):
    return pieces.astype(jnp.float32).reshape(UNITS, WIDE)


def body(
    q_hbm, k_hbm, v_hbm, step_hbm, fw_hbm, len_hbm, out_ref,
    q_ref, step_ref, fw_ref, len_ref, kx, vx, acc, top, mass, told, kid, qid,
    cross, wo, part, inbox, piece_out, piece_in, col_out, col_in, nw,
    sems, half_sems, halo_sems, load_sems,
):
    tok = lax.axis_index("tok")
    mem = lax.axis_index("mem")
    n_tok = lax.axis_size("tok")
    rows = q_ref.shape[0]
    mine = pl.ds(2 * mem, 2)
    core = lax.rem(tok, 2)
    other = 1 - core
    plane = tok // 8
    spot = lax.rem(tok, 8)
    level = spot // 2
    partner = tok + 1 - 2 * core
    right = lax.rem(tok + 1, n_tok)
    left = lax.rem(tok + n_tok - 1, n_tok)
    total_rows = n_tok * rows
    rate = 1.0 / math.sqrt(total_rows)

    def plane_at(d):
        across = lax.rem(plane // SIDE + d // SIDE, SIDE)
        return across * SIDE + lax.rem(lax.rem(plane, SIDE) + d % SIDE, SIDE)

    def plane_peer(d):
        return plane_at(d) * 8 + spot

    def column_peer(d):
        return plane * 8 + lax.rem(level + d, COLUMN) * 2 + core

    def send(src, dst, s_sem, r_sem, tok_id, mem_id=None):
        return pltpu.make_async_remote_copy(
            src_ref=src, dst_ref=dst, send_sem=s_sem, recv_sem=r_sem,
            device_id={"tok": tok_id, "mem": mem if mem_id is None else mem_id},
            device_id_type=MESH,
        )

    middle = pl.ds(rows, rows)
    loads = [
        pltpu.make_async_copy(src, dst, load_sems.at[n])
        for n, (src, dst) in enumerate((
            (fw_hbm.at[mine], fw_ref),
            (k_hbm, kx.at[middle]),
            (v_hbm, vx.at[middle]),
            (step_hbm, step_ref),
            (len_hbm, len_ref),
            (q_hbm, q_ref),
        ))
    ]
    for load in loads:
        load.start()

    barrier = pltpu.get_barrier_semaphore()

    def greet(tok_id, mem_id):
        pl.semaphore_signal(
            barrier, inc=1, device_id={"tok": tok_id, "mem": mem_id}, device_id_type=MESH
        )

    greet(partner, mem)
    greet(tok, 1 - mem)
    greet(left, mem)
    greet(right, mem)

    for d in FAR_FIRST:
        greet(plane_peer(d), mem)

    @pl.loop(1, COLUMN)
    def _(d):
        greet(column_peer(d), mem)

    for load in loads[:4]:
        load.wait()

    def grads(j, wb):
        lanes = pl.ds(pl.multiple_of(j * DM, DM), DM)
        kj = kx[pl.ds(rows, rows), lanes]
        vj = vx[pl.ds(rows, rows), lanes]
        step = step_ref[pl.ds(2 * mem + j, 1), :]
        pre = dot(jnp.concatenate([wb[:, :DM], wb[:, DM : 2 * DM]], axis=0), kj, NT)
        gate, up = pre[:UNITS], pre[UNITS:]
        back = -dot(wb[:, 2 * DM :], vj, NT) * step
        sig = jax.nn.sigmoid(gate)
        swish = gate * sig
        slope = sig * (1.0 + gate * (1.0 - sig))
        hidden = (swish * up * step).astype(jnp.bfloat16)
        gate_back = (back * up * slope).astype(jnp.bfloat16)
        up_back = (back * swish).astype(jnp.bfloat16)
        both = dot(jnp.concatenate([gate_back, up_back], axis=0), kj, NN)
        out = -dot(hidden, vj, NN)
        return jnp.concatenate([both[:UNITS], both[UNITS:], out], axis=1).reshape(
            PLANE, PIECE, WIDE
        )

    def core_start(half, value):
        part[half, 0] = value.astype(jnp.bfloat16)
        copy = send(part.at[half, 0], inbox.at[half], half_sems.at[half, 0], half_sems.at[half, 1], partner)
        copy.start()
        return copy

    def scatter_start(half, copy, own):
        copy.wait_recv()
        total = own[...] + inbox[half].astype(jnp.float32)
        own[...] = total
        part[half, 1] = total.astype(jnp.bfloat16)

        for d in FAR_FIRST:
            to = plane_at(d)
            send(
                part.at[half, 1, to], piece_in.at[half, d - 1],
                half_sems.at[half, 2], half_sems.at[half, 3], to * 8 + spot,
            ).start()

    def whole(half):
        return send(
            part.at[half, 1, pl.ds(0, PLANE - 1)], piece_in.at[half],
            half_sems.at[half, 2], half_sems.at[half, 3], plane_peer(1),
        )

    def column_start(half, own):
        whole(half).wait_recv()
        total = own[plane]
        for d in range(PLANE - 1):
            total = total + piece_in[half, d].astype(jnp.float32)
        col_out[half] = total.astype(jnp.bfloat16)

        @pl.loop(1, COLUMN)
        def _(d):
            send(
                col_out.at[half], col_in.at[half, d - 1],
                half_sems.at[half, 4], half_sems.at[half, 5], column_peer(d),
            ).start()

    def column_whole(half):
        return send(
            col_in.at[half], col_in.at[half],
            half_sems.at[half, 4], half_sems.at[half, 5], column_peer(1),
        )

    def update(half, before):
        column_whole(half).wait_recv()
        total = col_out[half].astype(jnp.float32)
        for d in range(COLUMN - 1):
            total = total + col_in[half, d].astype(jnp.float32)
        stepped = before - total * rate
        blocks = []
        for b in range(3):
            old = before[:, b * DM : (b + 1) * DM]
            new = stepped[:, b * DM : (b + 1) * DM]
            old_norm = jnp.sqrt(jnp.sum(old * old, axis=1, keepdims=True))
            new_norm = jnp.sqrt(jnp.sum(new * new, axis=1, keepdims=True) + norm_epsilon)
            blocks.append(new * (old_norm / new_norm))
        nw[half, core, plane] = jnp.concatenate(blocks, axis=1).astype(jnp.bfloat16)

        for d in FAR_FIRST:
            send(
                nw.at[half, core, plane], nw.at[half, core, plane],
                half_sems.at[half, 6], half_sems.at[half, 7], plane_peer(d),
            ).start()

    def gather_whole(half):
        return send(
            nw.at[half, core, pl.ds(0, PLANE - 1)], nw.at[half, core, pl.ds(0, PLANE - 1)],
            half_sems.at[half, 6], half_sems.at[half, 7], plane_peer(1),
        )

    def swap_start(half):
        gather_whole(half).wait_recv()
        copy = send(
            nw.at[half, core], nw.at[half, core],
            half_sems.at[half, 8], half_sems.at[half, 9], partner,
        )
        copy.start()
        return copy

    own_l, own_o = piece_out.at[0], piece_out.at[1]

    away = grads(other, fw_ref[other].astype(jnp.bfloat16))
    own_l[...] = grads(core, fw_ref[core].astype(jnp.bfloat16))

    pl.semaphore_wait(barrier, PLANE - 1 + COLUMN - 1 + 4)

    first = pl.ds(pl.multiple_of(plane * PIECE, PIECE), PIECE)
    crossing = send(
        fw_hbm.at[2 * (1 - mem) + core, first], cross,
        sems.at[2], sems.at[3], tok, 1 - mem,
    )
    crossing.start()
    core_l = core_start(0, away)

    blocks = rows // HD
    halos = []
    for n in range(2 * blocks):
        buf = (kx, vx)[n % 2]
        near, far = n // 2, blocks - 1 - n // 2
        halos.append((
            send(
                buf.at[pl.ds(rows + far * HD, HD)], buf.at[pl.ds(far * HD, HD)],
                halo_sems.at[n, 0], halo_sems.at[n, 1], right,
            ),
            send(
                buf.at[pl.ds(rows + near * HD, HD)], buf.at[pl.ds(2 * rows + near * HD, HD)],
                halo_sems.at[n, 2], halo_sems.at[n, 3], left,
            ),
        ))

    def halo_start(n):
        for copy in halos[n]:
            copy.start()

    halo_start(0)
    halo_start(1)

    for load in loads[4:]:
        load.wait()
    count = len_ref.shape[1]
    lengths = len_ref[...].astype(jnp.float32)
    square = (count, count)
    down = lax.broadcasted_iota(jnp.int32, square, 0)
    along = lax.broadcasted_iota(jnp.int32, square, 1)
    spread = jnp.broadcast_to(lengths, square)
    ends_col = jnp.sum(jnp.where(along <= down, spread, 0.0), axis=1, keepdims=True)
    len_col = jnp.sum(jnp.where(along == down, spread, 0.0), axis=1, keepdims=True)
    ends_row = jnp.sum(jnp.where(down <= along, len_col, 0.0), axis=0, keepdims=True)
    base = tok * rows
    spots = base - rows + lax.broadcasted_iota(jnp.int32, (1, 3 * rows), 1)
    spots_f = spots.astype(jnp.float32)
    key_views = jnp.sum(jnp.where(ends_col <= spots_f, 1.0, 0.0), axis=0, keepdims=True)
    kid[...] = jnp.where((spots >= 0) & (spots < total_rows), key_views, -1.0)
    rows_f = (base + lax.broadcasted_iota(jnp.int32, (rows, 1), 0)).astype(jnp.float32)
    query_views = jnp.sum(jnp.where(ends_row <= rows_f, 1.0, 0.0), axis=1, keepdims=True)
    qid[...] = jnp.broadcast_to(query_views, (rows, HD))

    scatter_start(0, core_l, own_l)
    halo_start(2)

    factor = 1.0 / math.sqrt(HD) * math.log2(math.e)
    heads = q_ref.shape[1] // HD

    def attend_own(start, stop):
        @pl.loop(start, stop)
        def _(i):
            here = pl.ds(pl.multiple_of(i * HD, HD), HD)
            same = qid[here, :1] == kid[:, rows : 2 * rows]
            for h in range(heads):
                lanes = slice(h * HD, (h + 1) * HD)
                scores = dot(q_ref[here, lanes], kx[middle, lanes], NT)
                scores = jnp.where(same, scores * factor, -1e30)
                peak = jnp.max(scores, axis=1, keepdims=True)
                weight = jnp.exp2(scores - peak)
                top[here, lanes] = jnp.broadcast_to(peak, (HD, HD))
                mass[here, lanes] = jnp.broadcast_to(
                    jnp.sum(weight, axis=1, keepdims=True), (HD, HD)
                )
                acc[here, lanes] = dot(weight.astype(jnp.bfloat16), vx[middle, lanes], NN)

    def attend_more(start, stop, first_key):
        keys = slice(first_key, first_key + HD)

        @pl.loop(start, stop)
        def _(i):
            here = pl.ds(pl.multiple_of(i * HD, HD), HD)
            same = qid[here, :] == kid[:, keys]
            for h in range(heads):
                lanes = slice(h * HD, (h + 1) * HD)
                scores = dot(q_ref[here, lanes], kx[keys, lanes], NT)
                scores = jnp.where(same, scores * factor, -1e30)
                before = top[here, lanes]
                peak = jnp.maximum(before, jnp.max(scores, axis=1, keepdims=True))
                weight = jnp.exp2(scores - peak)
                fade = jnp.exp2(before - peak)
                top[here, lanes] = peak
                mass[here, lanes] = mass[here, lanes] * fade + jnp.sum(
                    weight, axis=1, keepdims=True
                )
                acc[here, lanes] = acc[here, lanes] * fade + dot(
                    weight.astype(jnp.bfloat16), vx[keys, lanes], NN
                )

    def attend_halo(k):
        for n in (2 * k, 2 * k + 1):
            for copy in halos[n]:
                copy.wait_recv()
        attend_more(0, blocks - k, (blocks - 1 - k) * HD)
        attend_more(k, blocks, 2 * rows + k * HD)

    def read(half, j):
        w = flat(nw[half, j]).astype(jnp.bfloat16)
        qj = q_ref[:, j * DM : (j + 1) * DM]
        pre = dot(qj, jnp.concatenate([w[:, :DM], w[:, DM : 2 * DM]], axis=0), NT)
        gate, up = pre[:, :UNITS], pre[:, UNITS:]
        hidden = (gate * jax.nn.sigmoid(gate) * up).astype(jnp.bfloat16)
        return dot(hidden, w[:, 2 * DM :], NN)

    attend_own(0, blocks // 2)

    crossing.wait_recv()
    wo[core, plane] = cross[...].astype(jnp.bfloat16)
    for d in FAR_FIRST:
        send(
            wo.at[core, plane], wo.at[core, plane], sems.at[4], sems.at[5], plane_peer(d)
        ).start()
    halo_start(3)

    attend_own(blocks // 2, blocks)

    column_start(0, own_l)
    halo_start(4)

    gathered = send(
        wo.at[core, pl.ds(0, PLANE - 1)], wo.at[core, pl.ds(0, PLANE - 1)],
        sems.at[4], sems.at[5], plane_peer(1),
    )
    gathered.wait_recv()
    swapped = send(wo.at[core], wo.at[core], sems.at[6], sems.at[7], partner)
    swapped.start()
    halo_start(5)

    own_o[...] = grads(core, flat(wo[core]).astype(jnp.bfloat16))
    swapped.wait_recv()
    core_o = core_start(1, grads(other, flat(wo[other]).astype(jnp.bfloat16)))
    halo_start(6)

    update(0, fw_ref[core, first])
    scatter_start(1, core_o, own_o)
    halo_start(7)

    attend_halo(0)
    swap_l = swap_start(0)
    attend_halo(1)
    column_start(1, own_o)

    swap_l.wait_recv()
    for j in range(2):
        told[:, j * DM : (j + 1) * DM] = read(0, j)

    attend_halo(2)
    update(1, cross[...])
    attend_halo(3)
    acc[...] = acc[...] / mass[...] + told[...]
    swap_o = swap_start(1)
    swap_o.wait_recv()
    for j in range(2):
        lanes = slice(j * DM, (j + 1) * DM)
        out_ref[:, lanes] = (acc[:, lanes] + read(1, j)).astype(jnp.bfloat16)

    crossing.wait_send()
    gathered.wait_send()
    swapped.wait_send()
    for pair in halos:
        for copy in pair:
            copy.wait_send()
    for half, (first_copy, last_copy) in enumerate(((core_l, swap_l), (core_o, swap_o))):
        first_copy.wait_send()
        whole(half).wait_send()
        column_whole(half).wait_send()
        gather_whole(half).wait_send()
        last_copy.wait_send()


def on_device(queries, keys, values, step_sizes, fast_weights, view_lengths):
    rows, feats = queries.shape
    vmem = pl.BlockSpec(memory_space=pltpu.VMEM)
    hbm = pl.BlockSpec(memory_space=pl.ANY)
    bf, f32 = jnp.bfloat16, jnp.float32
    pieces = (PLANE, PIECE, WIDE)
    return pl.pallas_call(
        body,
        out_shape=jax.ShapeDtypeStruct((rows, feats), bf),
        in_specs=[hbm] * 6,
        out_specs=vmem,
        scratch_shapes=[
            pltpu.VMEM((rows, feats), bf),
            pltpu.VMEM(step_sizes.shape, f32),
            pltpu.VMEM((2,) + fast_weights.shape[1:], f32),
            pltpu.VMEM((1,) + view_lengths.shape, jnp.int32),
            pltpu.VMEM((3 * rows, feats), bf),
            pltpu.VMEM((3 * rows, feats), bf),
            pltpu.VMEM((rows, feats), f32),
            pltpu.VMEM((rows, feats), f32),
            pltpu.VMEM((rows, feats), f32),
            pltpu.VMEM((rows, feats), f32),
            pltpu.VMEM((1, 3 * rows), f32),
            pltpu.VMEM((rows, HD), f32),
            pltpu.VMEM((PIECE, WIDE), f32),
            pltpu.VMEM((2,) + pieces, bf),
            pltpu.VMEM((2, 2) + pieces, bf),
            pltpu.VMEM((2,) + pieces, bf),
            pltpu.VMEM((2,) + pieces, f32),
            pltpu.VMEM((2, PLANE - 1, PIECE, WIDE), bf),
            pltpu.VMEM((2, PIECE, WIDE), bf),
            pltpu.VMEM((2, COLUMN - 1, PIECE, WIDE), bf),
            pltpu.VMEM((2, 2) + pieces, bf),
            pltpu.SemaphoreType.DMA((8,)),
            pltpu.SemaphoreType.DMA((2, 10)),
            pltpu.SemaphoreType.DMA((2 * (rows // HD), 4)),
            pltpu.SemaphoreType.DMA((6,)),
        ],
        compiler_params=pltpu.CompilerParams(
            collective_id=0, has_side_effects=True, vmem_limit_bytes=VMEM_BYTES
        ),
    )(queries, keys, values, step_sizes, fast_weights, view_lengths.reshape(1, -1))


def solution(mesh):
    placed = (
        P("tok", "mem"),
        P("tok", "mem"),
        P("tok", "mem"),
        P(None, "tok"),
        P(None, "mem", None),
        P(),
    )
    return jax.shard_map(
        on_device, mesh=mesh, in_specs=placed, out_specs=P("tok", "mem"), check_vma=False
    )
```

```python
import math

import jax
import jax.numpy as jnp
from jax import lax
from jax.experimental import pallas as pl
from jax.experimental.pallas import tpu as pltpu
from jax.sharding import PartitionSpec as P

DM = 256
HD = 128
PLANE = 16
COLUMN = 4
UNITS = 128
PIECE = UNITS // PLANE
WIDE = 3 * DM
GROUP = 1
VMEM_BYTES = 40 * 1024 * 1024
MESH = pl.DeviceIdType.MESH
SIDE = 4
FAR_FIRST = sorted(
    (d for d in range(1, PLANE)),
    key=lambda d: -(min(d // SIDE, SIDE - d // SIDE) + min(d % SIDE, SIDE - d % SIDE)),
)
NT = (((1,), (1,)), ((), ()))
NN = (((1,), (0,)), ((), ()))

norm_epsilon = 1e-06


def dot(a, b, dims):
    return lax.dot_general(a, b, dims, preferred_element_type=jnp.float32)


def flat(pieces):
    return pieces.astype(jnp.float32).reshape(UNITS, WIDE)


def body(
    q_hbm, k_hbm, v_hbm, step_hbm, fw_hbm, len_hbm, out_ref,
    q_ref, step_ref, fw_ref, len_ref, kx, vx, acc, top, mass, told, kid, qid,
    cross, wo, part, inbox, piece_out, piece_in, col_out, col_in, nw,
    sems, half_sems, halo_sems, load_sems, hand_sems, plane_sems,
):
    tok = lax.axis_index("tok")
    mem = lax.axis_index("mem")
    n_tok = lax.axis_size("tok")
    rows = q_ref.shape[0]
    mine = pl.ds(2 * mem, 2)
    core = lax.rem(tok, 2)
    other = 1 - core
    plane = tok // 8
    spot = lax.rem(tok, 8)
    level = spot // 2
    partner = tok + 1 - 2 * core
    right = lax.rem(tok + 1, n_tok)
    left = lax.rem(tok + n_tok - 1, n_tok)
    total_rows = n_tok * rows
    rate = 1.0 / math.sqrt(total_rows)

    def plane_at(d):
        across = lax.rem(plane // SIDE + d // SIDE, SIDE)
        return across * SIDE + lax.rem(lax.rem(plane, SIDE) + d % SIDE, SIDE)

    def plane_peer(d):
        return plane_at(d) * 8 + spot

    def plane_from(d):
        across = lax.rem(plane // SIDE + SIDE - d // SIDE, SIDE)
        return across * SIDE + lax.rem(lax.rem(plane, SIDE) + SIDE - d % SIDE, SIDE)

    def column_peer(d):
        return plane * 8 + lax.rem(level + d, COLUMN) * 2 + core

    def send(src, dst, s_sem, r_sem, tok_id, mem_id=None):
        return pltpu.make_async_remote_copy(
            src_ref=src, dst_ref=dst, send_sem=s_sem, recv_sem=r_sem,
            device_id={"tok": tok_id, "mem": mem if mem_id is None else mem_id},
            device_id_type=MESH,
        )

    middle = pl.ds(rows, rows)
    loads = [
        pltpu.make_async_copy(src, dst, load_sems.at[n])
        for n, (src, dst) in enumerate((
            (fw_hbm.at[mine], fw_ref),
            (k_hbm, kx.at[middle]),
            (v_hbm, vx.at[middle]),
            (step_hbm, step_ref),
            (len_hbm, len_ref),
            (q_hbm, q_ref),
        ))
    ]
    for load in loads:
        load.start()

    barrier = pltpu.get_barrier_semaphore()

    def greet(tok_id, mem_id):
        pl.semaphore_signal(
            barrier, inc=1, device_id={"tok": tok_id, "mem": mem_id}, device_id_type=MESH
        )

    greet(partner, mem)
    greet(tok, 1 - mem)
    greet(left, mem)
    greet(right, mem)

    for d in FAR_FIRST:
        greet(plane_peer(d), mem)

    @pl.loop(1, COLUMN)
    def _(d):
        greet(column_peer(d), mem)

    for load in loads[:4]:
        load.wait()

    def grads(j, wb):
        lanes = pl.ds(pl.multiple_of(j * DM, DM), DM)
        kj = kx[pl.ds(rows, rows), lanes]
        vj = vx[pl.ds(rows, rows), lanes]
        step = step_ref[pl.ds(2 * mem + j, 1), :]
        pre = dot(jnp.concatenate([wb[:, :DM], wb[:, DM : 2 * DM]], axis=0), kj, NT)
        gate, up = pre[:UNITS], pre[UNITS:]
        back = -dot(wb[:, 2 * DM :], vj, NT) * step
        sig = jax.nn.sigmoid(gate)
        swish = gate * sig
        slope = sig * (1.0 + gate * (1.0 - sig))
        hidden = (swish * up * step).astype(jnp.bfloat16)
        gate_back = (back * up * slope).astype(jnp.bfloat16)
        up_back = (back * swish).astype(jnp.bfloat16)
        both = dot(jnp.concatenate([gate_back, up_back], axis=0), kj, NN)
        out = -dot(hidden, vj, NN)
        return jnp.concatenate([both[:UNITS], both[UNITS:], out], axis=1).reshape(
            PLANE, PIECE, WIDE
        )

    def core_start(half, value):
        part[half, 0] = value.astype(jnp.bfloat16)
        copy = send(part.at[half, 0], inbox.at[half], half_sems.at[half, 0], half_sems.at[half, 1], partner)
        copy.start()
        return copy

    def scatter_start(half, copy, own):
        copy.wait_recv()
        total = own[...] + inbox[half].astype(jnp.float32)
        own[...] = total
        part[half, 1] = total.astype(jnp.bfloat16)

        for d in FAR_FIRST:
            to = plane_at(d)
            send(
                part.at[half, 1, to], piece_in.at[half, d - 1],
                half_sems.at[half, 2], half_sems.at[half, 3], to * 8 + spot,
            ).start()

    def whole(half):
        return send(
            part.at[half, 1, pl.ds(0, PLANE - 1)], piece_in.at[half],
            half_sems.at[half, 2], half_sems.at[half, 3], plane_peer(1),
        )

    def column_start(half, own):
        whole(half).wait_recv()
        total = own[plane]
        for d in range(PLANE - 1):
            total = total + piece_in[half, d].astype(jnp.float32)
        col_out[half] = total.astype(jnp.bfloat16)

        @pl.loop(1, COLUMN)
        def _(d):
            send(
                col_out.at[half], col_in.at[half, d - 1],
                half_sems.at[half, 4], half_sems.at[half, 5], column_peer(d),
            ).start()

    def column_whole(half):
        return send(
            col_in.at[half], col_in.at[half],
            half_sems.at[half, 4], half_sems.at[half, 5], column_peer(1),
        )

    def update(half, before):
        column_whole(half).wait_recv()
        total = col_out[half].astype(jnp.float32)
        for d in range(COLUMN - 1):
            total = total + col_in[half, d].astype(jnp.float32)
        stepped = before - total * rate
        blocks = []
        for b in range(3):
            old = before[:, b * DM : (b + 1) * DM]
            new = stepped[:, b * DM : (b + 1) * DM]
            old_norm = jnp.sqrt(jnp.sum(old * old, axis=1, keepdims=True))
            new_norm = jnp.sqrt(jnp.sum(new * new, axis=1, keepdims=True) + norm_epsilon)
            blocks.append(new * (old_norm / new_norm))
        nw[half, core, plane] = jnp.concatenate(blocks, axis=1).astype(jnp.bfloat16)
        gather_start(half)

    def gathered_into(n):
        return wo.at[core] if n == 2 else nw.at[n, core]

    def plane_copy(n, piece, d):
        buf = gathered_into(n)
        return send(buf.at[piece], buf.at[piece], hand_sems.at[n, 0], plane_sems.at[n, d], plane_peer(d))

    def hand_copy(n, piece):
        buf = gathered_into(n)
        return send(buf.at[piece], buf.at[piece], hand_sems.at[n, 1], hand_sems.at[n, 2], partner)

    def hand_whole(n):
        buf = gathered_into(n)
        return send(buf, buf, hand_sems.at[n, 1], hand_sems.at[n, 2], partner)

    def gather_start(n):
        for d in FAR_FIRST:
            plane_copy(n, plane, d).start()
        hand_copy(n, plane).start()

    def gather_pass(n):
        for d in reversed(FAR_FIRST):
            piece = plane_from(d)
            plane_copy(n, piece, d).wait_recv()
            hand_copy(n, piece).start()

    def gather_sent(n):
        buf = gathered_into(n).at[pl.ds(0, PLANE - 1)]
        send(buf, buf, hand_sems.at[n, 0], plane_sems.at[n, 1], plane_peer(1)).wait_send()
        hand_whole(n).wait_send()

    own_l, own_o = piece_out.at[0], piece_out.at[1]

    away = grads(other, fw_ref[other].astype(jnp.bfloat16))
    own_l[...] = grads(core, fw_ref[core].astype(jnp.bfloat16))

    pl.semaphore_wait(barrier, PLANE - 1 + COLUMN - 1 + 4)

    first = pl.ds(pl.multiple_of(plane * PIECE, PIECE), PIECE)
    crossing = send(
        fw_hbm.at[2 * (1 - mem) + core, first], cross,
        sems.at[2], sems.at[3], tok, 1 - mem,
    )
    crossing.start()
    core_l = core_start(0, away)

    blocks = rows // HD
    halos = []
    for n in range(2 * blocks):
        buf = (kx, vx)[n % 2]
        near, far = n // 2, blocks - 1 - n // 2
        halos.append((
            send(
                buf.at[pl.ds(rows + far * HD, HD)], buf.at[pl.ds(far * HD, HD)],
                halo_sems.at[n, 0], halo_sems.at[n, 1], right,
            ),
            send(
                buf.at[pl.ds(rows + near * HD, HD)], buf.at[pl.ds(2 * rows + near * HD, HD)],
                halo_sems.at[n, 2], halo_sems.at[n, 3], left,
            ),
        ))

    def halo_start(n):
        for copy in halos[n]:
            copy.start()

    for n in range(3):
        halo_start(n)

    for load in loads[4:]:
        load.wait()
    count = len_ref.shape[1]
    lengths = len_ref[...].astype(jnp.float32)
    square = (count, count)
    down = lax.broadcasted_iota(jnp.int32, square, 0)
    along = lax.broadcasted_iota(jnp.int32, square, 1)
    spread = jnp.broadcast_to(lengths, square)
    ends_col = jnp.sum(jnp.where(along <= down, spread, 0.0), axis=1, keepdims=True)
    len_col = jnp.sum(jnp.where(along == down, spread, 0.0), axis=1, keepdims=True)
    ends_row = jnp.sum(jnp.where(down <= along, len_col, 0.0), axis=0, keepdims=True)
    base = tok * rows
    spots = base - rows + lax.broadcasted_iota(jnp.int32, (1, 3 * rows), 1)
    spots_f = spots.astype(jnp.float32)
    key_views = jnp.sum(jnp.where(ends_col <= spots_f, 1.0, 0.0), axis=0, keepdims=True)
    kid[...] = jnp.where((spots >= 0) & (spots < total_rows), key_views, -1.0)
    rows_f = (base + lax.broadcasted_iota(jnp.int32, (rows, 1), 0)).astype(jnp.float32)
    query_views = jnp.sum(jnp.where(ends_row <= rows_f, 1.0, 0.0), axis=1, keepdims=True)
    qid[...] = jnp.broadcast_to(query_views, (rows, HD))

    scatter_start(0, core_l, own_l)

    factor = 1.0 / math.sqrt(HD) * math.log2(math.e)
    heads = q_ref.shape[1] // HD

    ones = jnp.ones((HD, HD), jnp.bfloat16)

    def attend(here, spans, fresh):
        views = qid[here, :]
        same = [
            jnp.concatenate([views] * (size // HD), axis=1) == kid[:, start : start + size]
            for start, size in spans
        ]
        for head in range(0, heads, GROUP):
            group = [slice(h * HD, (h + 1) * HD) for h in range(head, head + GROUP)]
            scores = [
                [
                    jnp.where(
                        mask, dot(q_ref[here, lanes], kx[start : start + size, lanes], NT) * factor, -1e30
                    )
                    for mask, (start, size) in zip(same, spans)
                ]
                for lanes in group
            ]
            peaks, fades, sums = [], [], []
            for lanes, parts in zip(group, scores):
                best = parts[0][:, :HD]
                for part_scores in parts:
                    for n in range(0, part_scores.shape[1], HD):
                        best = jnp.maximum(best, part_scores[:, n : n + HD])
                peak = jnp.broadcast_to(jnp.max(best, axis=1, keepdims=True), (HD, HD))
                if not fresh:
                    before = top[here, lanes]
                    peak = jnp.maximum(peak, before)
                    fades.append(jnp.exp2(before - peak))
                peaks.append(peak)
            for lanes, parts, peak in zip(group, scores, peaks):
                total = None
                for part_scores, (start, size) in zip(parts, spans):
                    weight = jnp.exp2(
                        part_scores - jnp.concatenate([peak] * (size // HD), axis=1)
                    ).astype(jnp.bfloat16)
                    beside = jnp.concatenate(
                        [vx[start : start + size, lanes], jnp.concatenate([ones] * (size // HD), axis=0)],
                        axis=1,
                    )
                    term = dot(weight, beside, NN)
                    total = term if total is None else total + term
                sums.append(total)
            if not fresh:
                sums = [
                    total + fade_all * jnp.concatenate([acc[here, lanes], mass[here, lanes]], axis=1)
                    for total, lanes, fade_all in zip(
                        sums, group, [jnp.concatenate([fade, fade], axis=1) for fade in fades]
                    )
                ]
            for lanes, peak, total in zip(group, peaks, sums):
                top[here, lanes] = peak
                acc[here, lanes] = total[:, :HD]
                mass[here, lanes] = total[:, HD:]

    def attend_own(start, stop):
        @pl.loop(start, stop)
        def _(i):
            attend(pl.ds(pl.multiple_of(i * HD, HD), HD), [(rows, rows)], True)

    def attend_halo(first_chunk, last_chunk):
        for n in range(2 * first_chunk, 2 * last_chunk):
            for copy in halos[n]:
                copy.wait_recv()
        for i in range(blocks):
            low, high = max(i, blocks - last_chunk), blocks - first_chunk
            spans = [(low * HD, (high - low) * HD)] if high > low else []
            low, high = first_chunk, min(i + 1, last_chunk)
            spans += [(2 * rows + low * HD, (high - low) * HD)] if high > low else []
            attend(pl.ds(i * HD, HD), spans, False)

    def read(half, j):
        w = flat(nw[half, j]).astype(jnp.bfloat16)
        qj = q_ref[:, pl.ds(pl.multiple_of(j * DM, DM), DM)]
        pre = dot(qj, jnp.concatenate([w[:, :DM], w[:, DM : 2 * DM]], axis=0), NT)
        gate, up = pre[:, :UNITS], pre[:, UNITS:]
        hidden = (gate * jax.nn.sigmoid(gate) * up).astype(jnp.bfloat16)
        return dot(hidden, w[:, 2 * DM :], NN)

    attend_own(0, blocks // 2)

    crossing.wait_recv()
    wo[core, plane] = cross[...].astype(jnp.bfloat16)
    gather_start(2)

    attend_own(blocks // 2, blocks)

    column_start(0, own_l)
    halo_start(3)

    gather_pass(2)
    halo_start(4)

    own_o[...] = grads(core, flat(wo[core]).astype(jnp.bfloat16))
    hand_whole(2).wait_recv()
    core_o = core_start(1, grads(other, flat(wo[other]).astype(jnp.bfloat16)))
    halo_start(5)
    scatter_start(1, core_o, own_o)
    halo_start(6)

    update(0, fw_ref[core, first])
    attend_halo(0, 2)
    column_start(1, own_o)
    halo_start(7)
    gather_pass(0)

    hand_whole(0).wait_recv()
    for j in range(2):
        told[:, j * DM : (j + 1) * DM] = read(0, j)

    update(1, cross[...])
    attend_halo(2, 4)
    acc[...] = acc[...] / mass[...] + told[...]
    gather_pass(1)

    def finish(j):
        lanes = pl.ds(pl.multiple_of(j * DM, DM), DM)
        out_ref[:, lanes] = (acc[:, lanes] + read(1, j)).astype(jnp.bfloat16)

    finish(core)
    hand_whole(1).wait_recv()
    finish(other)

    crossing.wait_send()
    for pair in halos:
        for copy in pair:
            copy.wait_send()
    for half, first_copy in enumerate((core_l, core_o)):
        first_copy.wait_send()
        whole(half).wait_send()
        column_whole(half).wait_send()
    for n in range(3):
        gather_sent(n)


def on_device(queries, keys, values, step_sizes, fast_weights, view_lengths):
    rows, feats = queries.shape
    vmem = pl.BlockSpec(memory_space=pltpu.VMEM)
    hbm = pl.BlockSpec(memory_space=pltpu.HBM)
    bf, f32 = jnp.bfloat16, jnp.float32
    pieces = (PLANE, PIECE, WIDE)
    return pl.pallas_call(
        body,
        out_shape=jax.ShapeDtypeStruct((rows, feats), bf),
        in_specs=[hbm] * 6,
        out_specs=vmem,
        scratch_shapes=[
            pltpu.VMEM((rows, feats), bf),
            pltpu.VMEM(step_sizes.shape, f32),
            pltpu.VMEM((2,) + fast_weights.shape[1:], f32),
            pltpu.VMEM((1,) + view_lengths.shape, jnp.int32),
            pltpu.VMEM((3 * rows, feats), bf),
            pltpu.VMEM((3 * rows, feats), bf),
            pltpu.VMEM((rows, feats), f32),
            pltpu.VMEM((rows, feats), f32),
            pltpu.VMEM((rows, feats), f32),
            pltpu.VMEM((rows, feats), f32),
            pltpu.VMEM((1, 3 * rows), f32),
            pltpu.VMEM((rows, HD), f32),
            pltpu.VMEM((PIECE, WIDE), f32),
            pltpu.VMEM((2,) + pieces, bf),
            pltpu.VMEM((2, 2) + pieces, bf),
            pltpu.VMEM((2,) + pieces, bf),
            pltpu.VMEM((2,) + pieces, f32),
            pltpu.VMEM((2, PLANE - 1, PIECE, WIDE), bf),
            pltpu.VMEM((2, PIECE, WIDE), bf),
            pltpu.VMEM((2, COLUMN - 1, PIECE, WIDE), bf),
            pltpu.VMEM((2, 2) + pieces, bf),
            pltpu.SemaphoreType.DMA((4,)),
            pltpu.SemaphoreType.DMA((2, 6)),
            pltpu.SemaphoreType.DMA((2 * (rows // HD), 4)),
            pltpu.SemaphoreType.DMA((6,)),
            pltpu.SemaphoreType.DMA((3, 3)),
            pltpu.SemaphoreType.DMA((3, PLANE)),
        ],
        compiler_params=pltpu.CompilerParams(
            collective_id=0, has_side_effects=True, vmem_limit_bytes=VMEM_BYTES
        ),
    )(*[pltpu.with_memory_space_constraint(a, pltpu.HBM) for a in (queries, keys, values, step_sizes, fast_weights, view_lengths.reshape(1, -1))])


def solution(mesh):
    placed = (
        P("tok", "mem"),
        P("tok", "mem"),
        P("tok", "mem"),
        P(None, "tok"),
        P(None, "mem", None),
        P(),
    )
    return jax.shard_map(
        on_device, mesh=mesh, in_specs=placed, out_specs=P("tok", "mem"), check_vma=False
    )
```

```python
import math

import jax
import jax.numpy as jnp
from jax import lax
from jax.experimental import pallas as pl
from jax.experimental.pallas import tpu as pltpu
from jax.sharding import PartitionSpec as P

DM = 256
HD = 128
PLANE = 16
COLUMN = 4
UNITS = 128
PIECE = UNITS // PLANE
WIDE = 3 * DM
GROUP = 1
VMEM_BYTES = 40 * 1024 * 1024
MESH = pl.DeviceIdType.MESH
SIDE = 4
FAR_FIRST = sorted(
    (d for d in range(1, PLANE)),
    key=lambda d: -(min(d // SIDE, SIDE - d // SIDE) + min(d % SIDE, SIDE - d % SIDE)),
)
NT = (((1,), (1,)), ((), ()))
NN = (((1,), (0,)), ((), ()))

norm_epsilon = 1e-06


def dot(a, b, dims):
    return lax.dot_general(a, b, dims, preferred_element_type=jnp.float32)


def flat(pieces):
    return pieces.astype(jnp.float32).reshape(UNITS, WIDE)


def body(
    q_hbm, k_hbm, v_hbm, step_hbm, fw_hbm, len_hbm, out_ref,
    q_ref, step_ref, fw_ref, len_ref, kx, vx, acc, top, mass, told, kid, qid,
    rows_out, rows_in, cast_out, cast_in, wo, part, inbox, piece_out, piece_in, col_out, col_in, nw,
    half_sems, halo_sems, load_sems, swap_sems, cross_sems,
):
    tok = lax.axis_index("tok")
    mem = lax.axis_index("mem")
    n_tok = lax.axis_size("tok")
    rows = q_ref.shape[0]
    mine = pl.ds(2 * mem, 2)
    first = pl.ds(pl.multiple_of(lax.axis_index("tok") // 8 * PIECE, PIECE), PIECE)
    core = lax.rem(tok, 2)
    other = 1 - core
    plane = tok // 8
    spot = lax.rem(tok, 8)
    level = spot // 2
    partner = tok + 1 - 2 * core
    right = lax.rem(tok + 1, n_tok)
    left = lax.rem(tok + n_tok - 1, n_tok)
    total_rows = n_tok * rows
    rate = 1.0 / math.sqrt(total_rows)

    def plane_at(d):
        across = lax.rem(plane // SIDE + d // SIDE, SIDE)
        return across * SIDE + lax.rem(lax.rem(plane, SIDE) + d % SIDE, SIDE)

    def plane_peer(d):
        return plane_at(d) * 8 + spot

    def column_peer(d):
        return plane * 8 + lax.rem(level + d, COLUMN) * 2 + core

    def beyond(to_level):
        return plane * 8 + to_level * 2 + core

    edge = (level == 0) | (level == COLUMN - 1)

    def send(src, dst, s_sem, r_sem, tok_id, mem_id=None):
        return pltpu.make_async_remote_copy(
            src_ref=src, dst_ref=dst, send_sem=s_sem, recv_sem=r_sem,
            device_id={"tok": tok_id, "mem": mem if mem_id is None else mem_id},
            device_id_type=MESH,
        )

    middle = pl.ds(rows, rows)
    loads = [
        pltpu.make_async_copy(src, dst, load_sems.at[n])
        for n, (src, dst) in enumerate((
            (fw_hbm.at[mine], fw_ref),
            (k_hbm, kx.at[middle]),
            (v_hbm, vx.at[middle]),
            (step_hbm, step_ref),
            (fw_hbm.at[2 * (1 - mem) + core, first], rows_out),
            (len_hbm, len_ref),
            (q_hbm, q_ref),
        ))
    ]
    for load in loads:
        load.start()

    barrier = pltpu.get_barrier_semaphore()

    def greet(tok_id, mem_id):
        pl.semaphore_signal(
            barrier, inc=1, device_id={"tok": tok_id, "mem": mem_id}, device_id_type=MESH
        )

    greet(partner, mem)
    greet(beyond(jnp.where(level < 2, COLUMN - 1, 0)), 1 - mem)
    greet(left, mem)
    greet(right, mem)

    for d in FAR_FIRST:
        greet(plane_peer(d), mem)

    @pl.loop(1, COLUMN)
    def _(d):
        greet(column_peer(d), mem)

    for load in loads[:5]:
        load.wait()

    def grads(j, wb):
        lanes = pl.ds(pl.multiple_of(j * DM, DM), DM)
        kj = kx[pl.ds(rows, rows), lanes]
        vj = vx[pl.ds(rows, rows), lanes]
        step = step_ref[pl.ds(2 * mem + j, 1), :]
        pre = dot(jnp.concatenate([wb[:, :DM], wb[:, DM : 2 * DM]], axis=0), kj, NT)
        gate, up = pre[:UNITS], pre[UNITS:]
        back = -dot(wb[:, 2 * DM :], vj, NT) * step
        sig = jax.nn.sigmoid(gate)
        swish = gate * sig
        slope = sig * (1.0 + gate * (1.0 - sig))
        hidden = (swish * up * step).astype(jnp.bfloat16)
        gate_back = (back * up * slope).astype(jnp.bfloat16)
        up_back = (back * swish).astype(jnp.bfloat16)
        both = dot(jnp.concatenate([gate_back, up_back], axis=0), kj, NN)
        out = -dot(hidden, vj, NN)
        return jnp.concatenate([both[:UNITS], both[UNITS:], out], axis=1).reshape(
            PLANE, PIECE, WIDE
        )

    def core_start(half, value):
        part[half, 0] = value.astype(jnp.bfloat16)
        copy = send(part.at[half, 0], inbox.at[half], half_sems.at[half, 0], half_sems.at[half, 1], partner)
        copy.start()
        return copy

    def scatter_start(half, copy, own):
        copy.wait_recv()
        total = own[...] + inbox[half].astype(jnp.float32)
        own[...] = total
        part[half, 1] = total.astype(jnp.bfloat16)

        for d in FAR_FIRST:
            to = plane_at(d)
            send(
                part.at[half, 1, to], piece_in.at[half, d - 1],
                half_sems.at[half, 2], half_sems.at[half, 3], to * 8 + spot,
            ).start()

    def whole(half):
        return send(
            part.at[half, 1, pl.ds(0, PLANE - 1)], piece_in.at[half],
            half_sems.at[half, 2], half_sems.at[half, 3], plane_peer(1),
        )

    def column_start(half, own):
        whole(half).wait_recv()
        total = own[plane]
        for d in range(PLANE - 1):
            total = total + piece_in[half, d].astype(jnp.float32)
        col_out[half] = total.astype(jnp.bfloat16)

        @pl.loop(1, COLUMN)
        def _(d):
            send(
                col_out.at[half], col_in.at[half, d - 1],
                half_sems.at[half, 4], half_sems.at[half, 5], column_peer(d),
            ).start()

    def column_whole(half):
        return send(
            col_in.at[half], col_in.at[half],
            half_sems.at[half, 4], half_sems.at[half, 5], column_peer(1),
        )

    def update(half, before):
        column_whole(half).wait_recv()
        total = col_out[half].astype(jnp.float32)
        for d in range(COLUMN - 1):
            total = total + col_in[half, d].astype(jnp.float32)
        stepped = before - total * rate
        blocks = []
        for b in range(3):
            old = before[:, b * DM : (b + 1) * DM]
            new = stepped[:, b * DM : (b + 1) * DM]
            old_norm = jnp.sqrt(jnp.sum(old * old, axis=1, keepdims=True))
            new_norm = jnp.sqrt(jnp.sum(new * new, axis=1, keepdims=True) + norm_epsilon)
            blocks.append(new * (old_norm / new_norm))
        nw[half, core, plane] = jnp.concatenate(blocks, axis=1).astype(jnp.bfloat16)
        gather_start(half)

    def gathered_into(n):
        return wo.at[core] if n == 2 else nw.at[n, core]

    def gather_start(n):
        buf = gathered_into(n)
        for d in FAR_FIRST:
            send(
                buf.at[plane], buf.at[plane], swap_sems.at[n, 0], swap_sems.at[n, 1], plane_peer(d)
            ).start()

    def gather_whole(n):
        buf = gathered_into(n).at[pl.ds(0, PLANE - 1)]
        return send(buf, buf, swap_sems.at[n, 0], swap_sems.at[n, 1], plane_peer(1))

    def swap_whole(n):
        buf = gathered_into(n)
        return send(buf, buf, swap_sems.at[n, 2], swap_sems.at[n, 3], partner)

    def swap_start(n):
        gather_whole(n).wait_recv()
        swap_whole(n).start()

    own_l, own_o = piece_out.at[0], piece_out.at[1]

    away = grads(other, fw_ref[other].astype(jnp.bfloat16))
    own_l[...] = grads(core, fw_ref[core].astype(jnp.bfloat16))

    cast_out[...] = rows_out[...].astype(jnp.bfloat16)

    pl.semaphore_wait(barrier, PLANE - 1 + COLUMN - 1 + 3 + jnp.where(edge, 2, 0))

    def crossing(n, hop):
        to_level = jnp.where(level == 0, COLUMN - 1 - hop, hop)
        src, dst = ((cast_out, cast_in), (rows_out, rows_in))[n]
        return send(
            src, dst, cross_sems.at[n, hop], cross_sems.at[n, 2], beyond(to_level), 1 - mem
        )

    @pl.when(edge)
    def _():
        for hop in range(2):
            crossing(0, hop).start()

    core_l = core_start(0, away)

    blocks = rows // HD
    halos = []
    for n in range(2 * blocks):
        buf = (kx, vx)[n % 2]
        near, far = n // 2, blocks - 1 - n // 2
        halos.append((
            send(
                buf.at[pl.ds(rows + far * HD, HD)], buf.at[pl.ds(far * HD, HD)],
                halo_sems.at[n, 0], halo_sems.at[n, 1], right,
            ),
            send(
                buf.at[pl.ds(rows + near * HD, HD)], buf.at[pl.ds(2 * rows + near * HD, HD)],
                halo_sems.at[n, 2], halo_sems.at[n, 3], left,
            ),
        ))

    def halo_start(n):
        for copy in halos[n]:
            copy.start()


    for n in range(0, 1):
        halo_start(n)
    for load in loads[5:]:
        load.wait()
    count = len_ref.shape[1]
    lengths = len_ref[...].astype(jnp.float32)
    square = (count, count)
    down = lax.broadcasted_iota(jnp.int32, square, 0)
    along = lax.broadcasted_iota(jnp.int32, square, 1)
    spread = jnp.broadcast_to(lengths, square)
    ends_col = jnp.sum(jnp.where(along <= down, spread, 0.0), axis=1, keepdims=True)
    len_col = jnp.sum(jnp.where(along == down, spread, 0.0), axis=1, keepdims=True)
    ends_row = jnp.sum(jnp.where(down <= along, len_col, 0.0), axis=0, keepdims=True)
    base = tok * rows
    spots = base - rows + lax.broadcasted_iota(jnp.int32, (1, 3 * rows), 1)
    spots_f = spots.astype(jnp.float32)
    key_views = jnp.sum(jnp.where(ends_col <= spots_f, 1.0, 0.0), axis=0, keepdims=True)
    kid[...] = jnp.where((spots >= 0) & (spots < total_rows), key_views, -1.0)
    rows_f = (base + lax.broadcasted_iota(jnp.int32, (rows, 1), 0)).astype(jnp.float32)
    query_views = jnp.sum(jnp.where(ends_row <= rows_f, 1.0, 0.0), axis=1, keepdims=True)
    qid[...] = jnp.broadcast_to(query_views, (rows, HD))

    scatter_start(0, core_l, own_l)
    for n in range(1, 3):
        halo_start(n)

    factor = 1.0 / math.sqrt(HD) * math.log2(math.e)
    heads = q_ref.shape[1] // HD

    ones = jnp.ones((HD, HD), jnp.bfloat16)

    def attend(here, spans, fresh):
        views = qid[here, :]
        same = [
            jnp.concatenate([views] * (size // HD), axis=1) == kid[:, start : start + size]
            for start, size in spans
        ]
        for head in range(0, heads, GROUP):
            group = [slice(h * HD, (h + 1) * HD) for h in range(head, head + GROUP)]
            scores = [
                [
                    jnp.where(
                        mask, dot(q_ref[here, lanes], kx[start : start + size, lanes], NT) * factor, -1e30
                    )
                    for mask, (start, size) in zip(same, spans)
                ]
                for lanes in group
            ]
            peaks, fades, sums = [], [], []
            for lanes, parts in zip(group, scores):
                best = parts[0][:, :HD]
                for part_scores in parts:
                    for n in range(0, part_scores.shape[1], HD):
                        best = jnp.maximum(best, part_scores[:, n : n + HD])
                peak = jnp.broadcast_to(jnp.max(best, axis=1, keepdims=True), (HD, HD))
                if not fresh:
                    before = top[here, lanes]
                    peak = jnp.maximum(peak, before)
                    fades.append(jnp.exp2(before - peak))
                peaks.append(peak)
            for lanes, parts, peak in zip(group, scores, peaks):
                total = None
                for part_scores, (start, size) in zip(parts, spans):
                    weight = jnp.exp2(
                        part_scores - jnp.concatenate([peak] * (size // HD), axis=1)
                    ).astype(jnp.bfloat16)
                    beside = jnp.concatenate(
                        [vx[start : start + size, lanes], jnp.concatenate([ones] * (size // HD), axis=0)],
                        axis=1,
                    )
                    term = dot(weight, beside, NN)
                    total = term if total is None else total + term
                sums.append(total)
            if not fresh:
                sums = [
                    total + fade_all * jnp.concatenate([acc[here, lanes], mass[here, lanes]], axis=1)
                    for total, lanes, fade_all in zip(
                        sums, group, [jnp.concatenate([fade, fade], axis=1) for fade in fades]
                    )
                ]
            for lanes, peak, total in zip(group, peaks, sums):
                top[here, lanes] = peak
                acc[here, lanes] = total[:, :HD]
                mass[here, lanes] = total[:, HD:]

    def attend_own(start, stop):
        @pl.loop(start, stop)
        def _(i):
            attend(pl.ds(pl.multiple_of(i * HD, HD), HD), [(rows, rows)], True)

    def attend_halo(first_chunk, last_chunk):
        for n in range(2 * first_chunk, 2 * last_chunk):
            for copy in halos[n]:
                copy.wait_recv()
        for i in range(blocks):
            low, high = max(i, blocks - last_chunk), blocks - first_chunk
            spans = [(low * HD, (high - low) * HD)] if high > low else []
            low, high = first_chunk, min(i + 1, last_chunk)
            spans += [(2 * rows + low * HD, (high - low) * HD)] if high > low else []
            if spans:
                attend(pl.ds(i * HD, HD), spans, False)

    def lanes_of(j):
        return pl.ds(pl.multiple_of(j * DM, DM), DM)

    def read(half, j):
        w = flat(nw[half, j]).astype(jnp.bfloat16)
        qj = q_ref[:, lanes_of(j)]
        pre = dot(qj, jnp.concatenate([w[:, :DM], w[:, DM : 2 * DM]], axis=0), NT)
        gate, up = pre[:, :UNITS], pre[:, UNITS:]
        hidden = (gate * jax.nn.sigmoid(gate) * up).astype(jnp.bfloat16)
        return dot(hidden, w[:, 2 * DM :], NN)

    crossing(0, 0).wait_recv()
    wo[core, plane] = cast_in[...]
    gather_start(2)
    for n in range(3, 7):
        halo_start(n)

    attend_own(0, blocks)

    column_start(0, own_l)
    for n in range(7, 8):
        halo_start(n)

    @pl.when(edge)
    def _():
        for hop in range(2):
            crossing(1, hop).start()

    swap_start(2)
    own_o[...] = grads(core, flat(wo[core]).astype(jnp.bfloat16))
    swap_whole(2).wait_recv()
    core_o = core_start(1, grads(other, flat(wo[other]).astype(jnp.bfloat16)))
    scatter_start(1, core_o, own_o)

    attend_halo(0, 1)
    column_start(1, own_o)
    update(0, fw_ref[core, first])
    crossing(1, 0).wait_recv()
    update(1, rows_in[...])
    attend_halo(1, 2)

    swap_start(0)
    told[:, lanes_of(core)] = read(0, core)
    swap_whole(0).wait_recv()
    told[:, lanes_of(other)] = read(0, other)

    swap_start(1)
    attend_halo(2, 4)
    told[:, lanes_of(core)] += read(1, core)
    swap_whole(1).wait_recv()
    told[:, lanes_of(other)] += read(1, other)
    out_ref[...] = (acc[...] / mass[...] + told[...]).astype(jnp.bfloat16)

    @pl.when(edge)
    def _():
        for n in range(2):
            for hop in range(2):
                crossing(n, hop).wait_send()

    for pair in halos:
        for copy in pair:
            copy.wait_send()
    for half, first_copy in enumerate((core_l, core_o)):
        first_copy.wait_send()
        whole(half).wait_send()
        column_whole(half).wait_send()
    for n in range(3):
        gather_whole(n).wait_send()
        swap_whole(n).wait_send()


def on_device(queries, keys, values, step_sizes, fast_weights, view_lengths):
    rows, feats = queries.shape
    vmem = pl.BlockSpec(memory_space=pltpu.VMEM)
    hbm = pl.BlockSpec(memory_space=pltpu.HBM)
    bf, f32 = jnp.bfloat16, jnp.float32
    pieces = (PLANE, PIECE, WIDE)
    return pl.pallas_call(
        body,
        out_shape=jax.ShapeDtypeStruct((rows, feats), bf),
        in_specs=[hbm] * 6,
        out_specs=vmem,
        scratch_shapes=[
            pltpu.VMEM((rows, feats), bf),
            pltpu.VMEM(step_sizes.shape, f32),
            pltpu.VMEM((2,) + fast_weights.shape[1:], f32),
            pltpu.VMEM((1,) + view_lengths.shape, jnp.int32),
            pltpu.VMEM((3 * rows, feats), bf),
            pltpu.VMEM((3 * rows, feats), bf),
            pltpu.VMEM((rows, feats), f32),
            pltpu.VMEM((rows, feats), f32),
            pltpu.VMEM((rows, feats), f32),
            pltpu.VMEM((rows, feats), f32),
            pltpu.VMEM((1, 3 * rows), f32),
            pltpu.VMEM((rows, HD), f32),
            pltpu.VMEM((PIECE, WIDE), f32),
            pltpu.VMEM((PIECE, WIDE), f32),
            pltpu.VMEM((PIECE, WIDE), bf),
            pltpu.VMEM((PIECE, WIDE), bf),
            pltpu.VMEM((2,) + pieces, bf),
            pltpu.VMEM((2, 2) + pieces, bf),
            pltpu.VMEM((2,) + pieces, bf),
            pltpu.VMEM((2,) + pieces, f32),
            pltpu.VMEM((2, PLANE - 1, PIECE, WIDE), bf),
            pltpu.VMEM((2, PIECE, WIDE), bf),
            pltpu.VMEM((2, COLUMN - 1, PIECE, WIDE), bf),
            pltpu.VMEM((2, 2) + pieces, bf),
            pltpu.SemaphoreType.DMA((2, 6)),
            pltpu.SemaphoreType.DMA((2 * (rows // HD), 4)),
            pltpu.SemaphoreType.DMA((7,)),
            pltpu.SemaphoreType.DMA((3, 4)),
            pltpu.SemaphoreType.DMA((2, 3)),
        ],
        compiler_params=pltpu.CompilerParams(
            collective_id=0, has_side_effects=True, vmem_limit_bytes=VMEM_BYTES
        ),
    )(*[pltpu.with_memory_space_constraint(a, pltpu.HBM) for a in (queries, keys, values, step_sizes, fast_weights, view_lengths.reshape(1, -1))])


def solution(mesh):
    placed = (
        P("tok", "mem"),
        P("tok", "mem"),
        P("tok", "mem"),
        P(None, "tok"),
        P(None, "mem", None),
        P(),
    )
    return jax.shard_map(
        on_device, mesh=mesh, in_specs=placed, out_specs=P("tok", "mem"), check_vma=False
    )
```

```python
import math

import jax
import jax.numpy as jnp
from jax import lax
from jax.experimental import pallas as pl
from jax.experimental.pallas import tpu as pltpu
from jax.sharding import PartitionSpec as P

DM = 256
HD = 128
PLANE = 16
COLUMN = 4
UNITS = 128
PIECE = UNITS // PLANE
WIDE = 3 * DM
GROUP = 1
VMEM_BYTES = 40 * 1024 * 1024
MESH = pl.DeviceIdType.MESH
SIDE = 4
FAR_FIRST = sorted(
    (d for d in range(1, PLANE)),
    key=lambda d: -(min(d // SIDE, SIDE - d // SIDE) + min(d % SIDE, SIDE - d % SIDE)),
)
NT = (((1,), (1,)), ((), ()))
NN = (((1,), (0,)), ((), ()))

norm_epsilon = 1e-06


def dot(a, b, dims):
    return lax.dot_general(a, b, dims, preferred_element_type=jnp.float32)


def flat(pieces):
    return pieces.astype(jnp.float32).reshape(UNITS, WIDE)


def body(
    q_hbm, k_hbm, v_hbm, step_hbm, fw_hbm, len_hbm, out_ref,
    q_ref, step_ref, fw_ref, len_ref, kx, vx, acc, top, mass, told, kid, qid,
    rows_out, rows_in, cast_out, cast_in, wo, part, inbox, piece_out, piece_in, col_out, col_in, nw,
    half_sems, halo_sems, load_sems, swap_sems, cross_sems,
):
    tok = lax.axis_index("tok")
    mem = lax.axis_index("mem")
    n_tok = lax.axis_size("tok")
    rows = q_ref.shape[0]
    mine = pl.ds(2 * mem, 2)
    first = pl.ds(pl.multiple_of(lax.axis_index("tok") // 8 * PIECE, PIECE), PIECE)
    core = lax.rem(tok, 2)
    other = 1 - core
    plane = tok // 8
    spot = lax.rem(tok, 8)
    level = spot // 2
    partner = tok + 1 - 2 * core
    right = lax.rem(tok + 1, n_tok)
    left = lax.rem(tok + n_tok - 1, n_tok)
    total_rows = n_tok * rows
    rate = 1.0 / math.sqrt(total_rows)

    def plane_at(d):
        across = lax.rem(plane // SIDE + d // SIDE, SIDE)
        return across * SIDE + lax.rem(lax.rem(plane, SIDE) + d % SIDE, SIDE)

    def plane_peer(d):
        return plane_at(d) * 8 + spot

    def column_peer(d):
        return plane * 8 + lax.rem(level + d, COLUMN) * 2 + core

    def beyond(to_level):
        return plane * 8 + to_level * 2 + core

    edge = (level == 0) | (level == COLUMN - 1)

    def send(src, dst, s_sem, r_sem, tok_id, mem_id=None):
        return pltpu.make_async_remote_copy(
            src_ref=src, dst_ref=dst, send_sem=s_sem, recv_sem=r_sem,
            device_id={"tok": tok_id, "mem": mem if mem_id is None else mem_id},
            device_id_type=MESH,
        )

    middle = pl.ds(rows, rows)
    loads = [
        pltpu.make_async_copy(src, dst, load_sems.at[n])
        for n, (src, dst) in enumerate((
            (fw_hbm.at[mine], fw_ref),
            (k_hbm, kx.at[middle]),
            (v_hbm, vx.at[middle]),
            (step_hbm, step_ref),
            (fw_hbm.at[2 * (1 - mem) + core, first], rows_out),
            (len_hbm, len_ref),
            (q_hbm, q_ref),
        ))
    ]
    for load in loads:
        load.start()

    barrier = pltpu.get_barrier_semaphore()

    def greet(tok_id, mem_id):
        pl.semaphore_signal(
            barrier, inc=1, device_id={"tok": tok_id, "mem": mem_id}, device_id_type=MESH
        )

    greet(partner, mem)
    greet(beyond(jnp.where(level < 2, COLUMN - 1, 0)), 1 - mem)
    greet(left, mem)
    greet(right, mem)

    for d in FAR_FIRST:
        greet(plane_peer(d), mem)

    @pl.loop(1, COLUMN)
    def _(d):
        greet(column_peer(d), mem)

    for load in loads[:5]:
        load.wait()

    def grads(j, wb):
        lanes = pl.ds(pl.multiple_of(j * DM, DM), DM)
        kj = kx[pl.ds(rows, rows), lanes]
        vj = vx[pl.ds(rows, rows), lanes]
        step = step_ref[pl.ds(2 * mem + j, 1), :]
        pre = dot(jnp.concatenate([wb[:, :DM], wb[:, DM : 2 * DM]], axis=0), kj, NT)
        gate, up = pre[:UNITS], pre[UNITS:]
        back = -dot(wb[:, 2 * DM :], vj, NT) * step
        sig = jax.nn.sigmoid(gate)
        swish = gate * sig
        slope = sig * (1.0 + gate * (1.0 - sig))
        hidden = (swish * up * step).astype(jnp.bfloat16)
        gate_back = (back * up * slope).astype(jnp.bfloat16)
        up_back = (back * swish).astype(jnp.bfloat16)
        both = dot(jnp.concatenate([gate_back, up_back], axis=0), kj, NN)
        out = -dot(hidden, vj, NN)
        return jnp.concatenate([both[:UNITS], both[UNITS:], out], axis=1).reshape(
            PLANE, PIECE, WIDE
        )

    def core_start(half, value):
        part[half, 0] = value.astype(jnp.bfloat16)
        copy = send(part.at[half, 0], inbox.at[half], half_sems.at[half, 0], half_sems.at[half, 1], partner)
        copy.start()
        return copy

    def scatter_start(half, copy, own):
        copy.wait_recv()
        total = own[...] + inbox[half].astype(jnp.float32)
        own[...] = total
        part[half, 1] = total.astype(jnp.bfloat16)

        for d in FAR_FIRST:
            to = plane_at(d)
            send(
                part.at[half, 1, to], piece_in.at[half, d - 1],
                half_sems.at[half, 2], half_sems.at[half, 3], to * 8 + spot,
            ).start()

    def whole(half):
        return send(
            part.at[half, 1, pl.ds(0, PLANE - 1)], piece_in.at[half],
            half_sems.at[half, 2], half_sems.at[half, 3], plane_peer(1),
        )

    def column_start(half, own):
        whole(half).wait_recv()
        total = own[plane]
        for d in range(PLANE - 1):
            total = total + piece_in[half, d].astype(jnp.float32)
        col_out[half] = total.astype(jnp.bfloat16)

        @pl.loop(1, COLUMN)
        def _(d):
            send(
                col_out.at[half], col_in.at[half, d - 1],
                half_sems.at[half, 4], half_sems.at[half, 5], column_peer(d),
            ).start()

    def column_whole(half):
        return send(
            col_in.at[half], col_in.at[half],
            half_sems.at[half, 4], half_sems.at[half, 5], column_peer(1),
        )

    def update(half, before):
        column_whole(half).wait_recv()
        total = col_out[half].astype(jnp.float32)
        for d in range(COLUMN - 1):
            total = total + col_in[half, d].astype(jnp.float32)
        stepped = before - total * rate
        blocks = []
        for b in range(3):
            old = before[:, b * DM : (b + 1) * DM]
            new = stepped[:, b * DM : (b + 1) * DM]
            old_norm = jnp.sqrt(jnp.sum(old * old, axis=1, keepdims=True))
            new_norm = jnp.sqrt(jnp.sum(new * new, axis=1, keepdims=True) + norm_epsilon)
            blocks.append(new * (old_norm / new_norm))
        nw[half, core, plane] = jnp.concatenate(blocks, axis=1).astype(jnp.bfloat16)
        gather_start(half)

    def gathered_into(n):
        return wo.at[core] if n == 2 else nw.at[n, core]

    def gather_start(n):
        buf = gathered_into(n)
        for d in FAR_FIRST:
            send(
                buf.at[plane], buf.at[plane], swap_sems.at[n, 0], swap_sems.at[n, 1], plane_peer(d)
            ).start()

    def gather_whole(n):
        buf = gathered_into(n).at[pl.ds(0, PLANE - 1)]
        return send(buf, buf, swap_sems.at[n, 0], swap_sems.at[n, 1], plane_peer(1))

    def swap_whole(n):
        buf = gathered_into(n)
        return send(buf, buf, swap_sems.at[n, 2], swap_sems.at[n, 3], partner)

    def swap_start(n):
        gather_whole(n).wait_recv()
        swap_whole(n).start()

    own_l, own_o = piece_out.at[0], piece_out.at[1]

    away = grads(other, fw_ref[other].astype(jnp.bfloat16))
    own_l[...] = grads(core, fw_ref[core].astype(jnp.bfloat16))

    cast_out[...] = rows_out[...].astype(jnp.bfloat16)

    pl.semaphore_wait(barrier, PLANE - 1 + COLUMN - 1 + 3 + jnp.where(edge, 2, 0))

    def crossing(n, hop):
        to_level = jnp.where(level == 0, COLUMN - 1 - hop, hop)
        src, dst = ((cast_out, cast_in), (rows_out, rows_in))[n]
        return send(
            src, dst, cross_sems.at[n, hop], cross_sems.at[n, 2], beyond(to_level), 1 - mem
        )

    @pl.when(edge)
    def _():
        for hop in range(2):
            crossing(0, hop).start()


    blocks = rows // HD
    halos = []
    for n in range(2 * blocks):
        buf = (kx, vx)[n % 2]
        near, far = n // 2, blocks - 1 - n // 2
        halos.append((
            send(
                buf.at[pl.ds(rows + far * HD, HD)], buf.at[pl.ds(far * HD, HD)],
                halo_sems.at[n, 0], halo_sems.at[n, 1], right,
            ),
            send(
                buf.at[pl.ds(rows + near * HD, HD)], buf.at[pl.ds(2 * rows + near * HD, HD)],
                halo_sems.at[n, 2], halo_sems.at[n, 3], left,
            ),
        ))

    def halo_start(n):
        for copy in halos[n]:
            copy.start()


    for n in range(0, 1):
        halo_start(n)
    core_l = core_start(0, away)

    for load in loads[5:]:
        load.wait()
    count = len_ref.shape[1]
    lengths = len_ref[...].astype(jnp.float32)
    square = (count, count)
    down = lax.broadcasted_iota(jnp.int32, square, 0)
    along = lax.broadcasted_iota(jnp.int32, square, 1)
    spread = jnp.broadcast_to(lengths, square)
    ends_col = jnp.sum(jnp.where(along <= down, spread, 0.0), axis=1, keepdims=True)
    len_col = jnp.sum(jnp.where(along == down, spread, 0.0), axis=1, keepdims=True)
    ends_row = jnp.sum(jnp.where(down <= along, len_col, 0.0), axis=0, keepdims=True)
    base = tok * rows
    spots = base - rows + lax.broadcasted_iota(jnp.int32, (1, 3 * rows), 1)
    spots_f = spots.astype(jnp.float32)
    key_views = jnp.sum(jnp.where(ends_col <= spots_f, 1.0, 0.0), axis=0, keepdims=True)
    kid[...] = jnp.where((spots >= 0) & (spots < total_rows), key_views, -1.0)
    rows_f = (base + lax.broadcasted_iota(jnp.int32, (rows, 1), 0)).astype(jnp.float32)
    query_views = jnp.sum(jnp.where(ends_row <= rows_f, 1.0, 0.0), axis=1, keepdims=True)
    qid[...] = jnp.broadcast_to(query_views, (rows, HD))

    scatter_start(0, core_l, own_l)
    for n in range(1, 3):
        halo_start(n)

    factor = 1.0 / math.sqrt(HD) * math.log2(math.e)
    heads = q_ref.shape[1] // HD

    ones = jnp.ones((HD, HD), jnp.bfloat16)

    def attend(here, spans, fresh):
        views = qid[here, :]
        same = [
            jnp.concatenate([views] * (size // HD), axis=1) == kid[:, start : start + size]
            for start, size in spans
        ]
        for head in range(0, heads, GROUP):
            group = [slice(h * HD, (h + 1) * HD) for h in range(head, head + GROUP)]
            scores = [
                [
                    jnp.where(
                        mask, dot(q_ref[here, lanes], kx[start : start + size, lanes], NT) * factor, -1e30
                    )
                    for mask, (start, size) in zip(same, spans)
                ]
                for lanes in group
            ]
            peaks, fades, sums = [], [], []
            for lanes, parts in zip(group, scores):
                best = parts[0][:, :HD]
                for part_scores in parts:
                    for n in range(0, part_scores.shape[1], HD):
                        best = jnp.maximum(best, part_scores[:, n : n + HD])
                peak = jnp.broadcast_to(jnp.max(best, axis=1, keepdims=True), (HD, HD))
                if not fresh:
                    before = top[here, lanes]
                    peak = jnp.maximum(peak, before)
                    fades.append(jnp.exp2(before - peak))
                peaks.append(peak)
            for lanes, parts, peak in zip(group, scores, peaks):
                total = None
                for part_scores, (start, size) in zip(parts, spans):
                    weight = jnp.exp2(
                        part_scores - jnp.concatenate([peak] * (size // HD), axis=1)
                    ).astype(jnp.bfloat16)
                    beside = jnp.concatenate(
                        [vx[start : start + size, lanes], jnp.concatenate([ones] * (size // HD), axis=0)],
                        axis=1,
                    )
                    term = dot(weight, beside, NN)
                    total = term if total is None else total + term
                sums.append(total)
            if not fresh:
                sums = [
                    total + fade_all * jnp.concatenate([acc[here, lanes], mass[here, lanes]], axis=1)
                    for total, lanes, fade_all in zip(
                        sums, group, [jnp.concatenate([fade, fade], axis=1) for fade in fades]
                    )
                ]
            for lanes, peak, total in zip(group, peaks, sums):
                top[here, lanes] = peak
                acc[here, lanes] = total[:, :HD]
                mass[here, lanes] = total[:, HD:]

    def attend_own(start, stop):
        @pl.loop(start, stop)
        def _(i):
            attend(pl.ds(pl.multiple_of(i * HD, HD), HD), [(rows, rows)], True)

    def attend_halo(first_chunk, last_chunk):
        for n in range(2 * first_chunk, 2 * last_chunk):
            for copy in halos[n]:
                copy.wait_recv()
        for i in range(blocks):
            low, high = max(i, blocks - last_chunk), blocks - first_chunk
            spans = [(low * HD, (high - low) * HD)] if high > low else []
            low, high = first_chunk, min(i + 1, last_chunk)
            spans += [(2 * rows + low * HD, (high - low) * HD)] if high > low else []
            if spans:
                attend(pl.ds(i * HD, HD), spans, False)

    def lanes_of(j):
        return pl.ds(pl.multiple_of(j * DM, DM), DM)

    def read(half, j):
        w = flat(nw[half, j]).astype(jnp.bfloat16)
        qj = q_ref[:, lanes_of(j)]
        pre = dot(qj, jnp.concatenate([w[:, :DM], w[:, DM : 2 * DM]], axis=0), NT)
        gate, up = pre[:, :UNITS], pre[:, UNITS:]
        hidden = (gate * jax.nn.sigmoid(gate) * up).astype(jnp.bfloat16)
        return dot(hidden, w[:, 2 * DM :], NN)

    crossing(0, 0).wait_recv()
    wo[core, plane] = cast_in[...]
    gather_start(2)
    for n in range(3, 6):
        halo_start(n)

    attend_own(0, blocks)

    column_start(0, own_l)

    @pl.when(edge)
    def _():
        for hop in range(2):
            crossing(1, hop).start()

    swap_start(2)
    own_o[...] = grads(core, flat(wo[core]).astype(jnp.bfloat16))
    swap_whole(2).wait_recv()
    core_o = core_start(1, grads(other, flat(wo[other]).astype(jnp.bfloat16)))
    scatter_start(1, core_o, own_o)
    for n in range(6, 7):
        halo_start(n)

    attend_halo(0, 1)
    column_start(1, own_o)
    for n in range(7, 8):
        halo_start(n)
    update(0, fw_ref[core, first])
    crossing(1, 0).wait_recv()
    update(1, rows_in[...])
    attend_halo(1, 2)

    swap_start(0)
    told[:, lanes_of(core)] = read(0, core)
    swap_whole(0).wait_recv()
    told[:, lanes_of(other)] = read(0, other)

    swap_start(1)
    attend_halo(2, 3)
    told[:, lanes_of(core)] += read(1, core)
    swap_whole(1).wait_recv()
    told[:, lanes_of(other)] += read(1, other)
    attend_halo(3, 4)
    out_ref[...] = (acc[...] / mass[...] + told[...]).astype(jnp.bfloat16)

    @pl.when(edge)
    def _():
        for n in range(2):
            for hop in range(2):
                crossing(n, hop).wait_send()

    for pair in halos:
        for copy in pair:
            copy.wait_send()
    for half, first_copy in enumerate((core_l, core_o)):
        first_copy.wait_send()
        whole(half).wait_send()
        column_whole(half).wait_send()
    for n in range(3):
        gather_whole(n).wait_send()
        swap_whole(n).wait_send()


def on_device(queries, keys, values, step_sizes, fast_weights, view_lengths):
    rows, feats = queries.shape
    vmem = pl.BlockSpec(memory_space=pltpu.VMEM)
    hbm = pl.BlockSpec(memory_space=pltpu.HBM)
    bf, f32 = jnp.bfloat16, jnp.float32
    pieces = (PLANE, PIECE, WIDE)
    return pl.pallas_call(
        body,
        out_shape=jax.ShapeDtypeStruct((rows, feats), bf),
        in_specs=[hbm] * 6,
        out_specs=vmem,
        scratch_shapes=[
            pltpu.VMEM((rows, feats), bf),
            pltpu.VMEM(step_sizes.shape, f32),
            pltpu.VMEM((2,) + fast_weights.shape[1:], f32),
            pltpu.VMEM((1,) + view_lengths.shape, jnp.int32),
            pltpu.VMEM((3 * rows, feats), bf),
            pltpu.VMEM((3 * rows, feats), bf),
            pltpu.VMEM((rows, feats), f32),
            pltpu.VMEM((rows, feats), f32),
            pltpu.VMEM((rows, feats), f32),
            pltpu.VMEM((rows, feats), f32),
            pltpu.VMEM((1, 3 * rows), f32),
            pltpu.VMEM((rows, HD), f32),
            pltpu.VMEM((PIECE, WIDE), f32),
            pltpu.VMEM((PIECE, WIDE), f32),
            pltpu.VMEM((PIECE, WIDE), bf),
            pltpu.VMEM((PIECE, WIDE), bf),
            pltpu.VMEM((2,) + pieces, bf),
            pltpu.VMEM((2, 2) + pieces, bf),
            pltpu.VMEM((2,) + pieces, bf),
            pltpu.VMEM((2,) + pieces, f32),
            pltpu.VMEM((2, PLANE - 1, PIECE, WIDE), bf),
            pltpu.VMEM((2, PIECE, WIDE), bf),
            pltpu.VMEM((2, COLUMN - 1, PIECE, WIDE), bf),
            pltpu.VMEM((2, 2) + pieces, bf),
            pltpu.SemaphoreType.DMA((2, 6)),
            pltpu.SemaphoreType.DMA((2 * (rows // HD), 4)),
            pltpu.SemaphoreType.DMA((7,)),
            pltpu.SemaphoreType.DMA((3, 4)),
            pltpu.SemaphoreType.DMA((2, 3)),
        ],
        compiler_params=pltpu.CompilerParams(
            collective_id=0, has_side_effects=True, vmem_limit_bytes=VMEM_BYTES
        ),
    )(*[pltpu.with_memory_space_constraint(a, pltpu.HBM) for a in (queries, keys, values, step_sizes, fast_weights, view_lengths.reshape(1, -1))])


def solution(mesh):
    placed = (
        P("tok", "mem"),
        P("tok", "mem"),
        P("tok", "mem"),
        P(None, "tok"),
        P(None, "mem", None),
        P(),
    )
    return jax.shard_map(
        on_device, mesh=mesh, in_specs=placed, out_specs=P("tok", "mem"), check_vma=False
    )
```
